256 devices in a mesh: wide: 32 (over z, x), narrow: 8 (over y, core).
Axes of the slice: x: 4, y: 4, z: 8, core: 2. Of those that a mesh axis runs over, the one named last changes fastest.
Arguments:
- samples: bfloat16 [131072, 1024], P(('wide', 'narrow')), may hold values from -16 to 16
- centroid_table: bfloat16 [65536, 1024], P('wide', 'narrow'), may hold values from -6 to 6
- owner: int32 [65536], replicated, may hold values from 0 to 31, as said below
- slot: int32 [65536], replicated, may hold values from 0 to 2047, as said below
- assign: int32 [131072], P('wide'), may hold values from 0 to 65535, as said below
- codebook: float32 [8, 2048, 128], P('narrow'), may hold values from -16 to 16
Outputs:
- residual: bfloat16 [131072, 1024], P('wide', 'narrow')
- refined: float32 [8, 2048, 128], P('narrow')
The draws below stay inside these ranges and needn't reach their ends.
Inputs may be any that keep to these rules, and one draw needn't show every extreme that they name: owner and slot give each coarse centroid a distinct storage position owner * 2048 + slot. `slot`: see owner. `assign`: in each aligned block of 4096 rows (the rows of one index of wide), at most 256 rows have centroids with one owner, and some owner has exactly 256.
All inputs are finite; a program needn't handle non-finite values.
Results may differ from the reference program's by a relative error of at most 0.0079.
Values may be sent and summed in bfloat16 or wider, within the bound.
A program may use at most 64 MiB of HBM per device.

```python
import jax
import jax.numpy as jnp
from jax import lax

D = 1024
SUB = 128
K = 2048
SLOTS = 2048
ITERS = 2
M = 8
NLIST = 65536
GROUP = 4096
ROWS = 131072
CAP = 256


def placed_order(key):
    return jax.random.permutation(jax.random.fold_in(key, 11), NLIST).astype(jnp.int32)


def draw_owner(key, part):
    position = jnp.argsort(placed_order(key))
    return (position // SLOTS).astype(jnp.int32)


def draw_slot(key, part):
    position = jnp.argsort(placed_order(key))
    return (position % SLOTS).astype(jnp.int32)


def draw_assign(key, part):
    placed = placed_order(key)
    occupant_sequence = NLIST // SLOTS
    place_sequence = occupant_sequence * CAP

    def draw_group(cluster_draw_seed):
        frequent_draw_seed, extra_credit_seed, chair_draw_seed, blend_draw_seed, bucket_draw_seed = jax.random.split(cluster_draw_seed, 5)
        hottest = jax.random.randint(frequent_draw_seed, (), 0, occupant_sequence)
        occupant_extra_credit = jax.random.randint(extra_credit_seed, (occupant_sequence,), 0, 1024)
        place_occupant = jnp.arange(place_sequence, dtype=jnp.int32) // CAP
        place_merit = jax.random.randint(chair_draw_seed, (place_sequence,), 0, 1024) + occupant_extra_credit[place_occupant]
        place_merit = place_merit + (place_occupant == hottest).astype(jnp.int32) * 4096
        place_merit = place_merit * place_sequence + jnp.arange(place_sequence, dtype=jnp.int32)
        ranking = jnp.argsort(-place_merit)
        row_owner = place_occupant[ranking[:GROUP]]
        row_owner = row_owner[jax.random.permutation(blend_draw_seed, GROUP)]
        row_slot = jax.random.randint(bucket_draw_seed, (GROUP,), 0, SLOTS)
        return placed[row_owner * SLOTS + row_slot]
    group_keys = jax.random.split(jax.random.fold_in(key, 23), ROWS // GROUP)
    return jax.vmap(draw_group)(group_keys).reshape(ROWS).astype(jnp.int32)


def draw_codebook(key, part):
    key_base = jax.random.fold_in(jax.random.fold_in(key, 31), 0)
    base = jax.random.normal(key_base, (M, K, SUB), jnp.float32)
    return jnp.clip(base, -16.0, 16.0)


def draw_samples(key, part):
    key_base = jax.random.fold_in(jax.random.fold_in(key, 41), 0)
    base = jax.random.normal(key_base, (ROWS, D), jnp.float32)
    return jnp.clip(base, -16.0, 16.0).astype(jnp.bfloat16)


def shard_levels(rng, dims, cuts, least, largest):
    def one(dim, blocks):
        heights = jax.random.uniform(jax.random.fold_in(jax.random.fold_in(rng, 6), dim), (blocks,), jnp.float32, least / len(cuts), largest / len(cuts))
        return jnp.repeat(jnp.exp(heights), dims[dim] // blocks).reshape((-1,) + (1,) * (len(dims) - dim - 1))

    factor_of = one(*cuts[0])
    for cut in cuts[1:]:
        factor_of = factor_of * one(*cut)
    return factor_of


def scatter_about(key, extent, scale, most, cuts=(), kind=jnp.bfloat16):
    level = shard_levels(key, extent, cuts, -0.22, 0.18) if cuts else 1.0
    entries = jax.random.normal(key, extent, jnp.float32) * scale * level
    return jnp.minimum(jnp.maximum(entries, -most), most).astype(kind)


def setup_inputs(seed: int = 0) -> dict:
    keys = jax.random.split(jax.random.key(seed), 7)
    samples = draw_samples(jax.random.fold_in(keys[6], 71), 0)
    centroid_table = scatter_about(keys[1], (NLIST, D), 1.0, 6.0, ((0, 32), (1, 8)))
    owner = draw_owner(jax.random.fold_in(keys[6], 71), 0)
    slot = draw_slot(jax.random.fold_in(keys[6], 71), 0)
    assign = draw_assign(jax.random.fold_in(keys[6], 71), 0)
    codebook = draw_codebook(jax.random.fold_in(keys[6], 71), 0)
    return dict(samples=samples, centroid_table=centroid_table, owner=owner, slot=slot, assign=assign, codebook=codebook)


softness_level = 16.0
prior_weight = 1.0


def refine(space_rows, codewords):
    blocks = space_rows.reshape(ROWS // GROUP, GROUP, SUB)
    for iteration in range(ITERS):
        narrow_words = lax.optimization_barrier(codewords.astype(jnp.bfloat16)).astype(jnp.float32)
        codeword_norm_values = jnp.sum(codewords * codewords, axis=1)

        def block_step(running, row_block):
            values = row_block.astype(jnp.float32)
            inner_product_rows = jnp.dot(values, narrow_words.T, precision=lax.Precision.HIGHEST)
            score_matrix = (2.0 * inner_product_rows - codeword_norm_values[None, :]) / softness_level
            weights_soft = jax.nn.softmax(score_matrix, axis=1)
            rounded = lax.optimization_barrier(weights_soft.astype(jnp.bfloat16)).astype(jnp.float32)
            totals = running[0] + jnp.dot(rounded.T, values, precision=lax.Precision.HIGHEST)
            return (totals, running[1] + jnp.sum(rounded, axis=0)), None

        start = (jnp.zeros((K, SUB), jnp.float32), jnp.zeros((K,), jnp.float32))
        (totals, counts), ignored = lax.scan(block_step, start, blocks)
        codewords = (totals + prior_weight * codewords) / (counts[:, None] + prior_weight)
    return codewords


def reference(samples, centroid_table, owner, slot, assign, codebook):
    position = (owner[assign] * SLOTS + slot[assign]).astype(jnp.int32)
    centre = jnp.take(centroid_table, position, axis=0)
    residual = (samples.astype(jnp.float32) - centre.astype(jnp.float32)).astype(jnp.bfloat16)
    spaces = residual.reshape(ROWS, D // SUB, SUB).transpose(1, 0, 2)
    refined = lax.map(lambda inputs: refine(inputs[0], inputs[1]), (spaces, codebook))
    return residual, refined
```

```python
import functools
import math

import jax
import jax.numpy as jnp
from jax import lax
from jax.experimental import pallas as pl
from jax.experimental.pallas import tpu as pltpu
from jax.sharding import PartitionSpec as P

ITERS = 2
NZ, NX, NN = 8, 4, 8
NW = NZ * NX
CAP = 256
ROWS = 4096
K = 2048
SUB = 128
PART = 512
XK = K // NX
OWN = XK // NZ
BLK = 512
MESH = pl.DeviceIdType.MESH
f32, bf16, i32 = jnp.float32, jnp.bfloat16, jnp.int32


def iota(shape, dim):
    return lax.broadcasted_iota(i32, shape, dim)


def hot(mask):
    return jnp.where(mask, 1.0, 0.0).astype(bf16)


def nt(a, b):
    return lax.dot_general(a, b, (((1,), (1,)), ((), ())), preferred_element_type=f32)


def greet(peers):
    barrier = pltpu.get_barrier_semaphore()
    for peer in peers:
        pl.semaphore_signal(barrier, inc=1, device_id=peer, device_id_type=MESH)
    pl.semaphore_wait(barrier, len(peers))


def exchange_kernel(
    samples, table, lut, assign, out,
    samp, tabs, req, reqin, gs, gin, upper, codes, picked, centre,
    own_sem, s_send, s_recv, up_send, up_recv, dn_send, dn_recv,
    q_send, q_recv, g_send, g_recv,
):
    w = lax.axis_index("wide")
    n = lax.axis_index("narrow")
    z = w // NX
    x = lax.rem(w, NX)

    def at_zx(zz, xx):
        return {"wide": lax.rem(zz + NZ, NZ) * NX + lax.rem(xx + NX, NX)}

    xpeers = [at_zx(z, x + d) for d in range(1, NX)]
    npeers = [{"narrow": lax.rem(n + d, NN)} for d in range(1, NN)]
    above, below = at_zx(z + 1, x), at_zx(z - 1, x)
    greet([above, below] + xpeers + npeers)

    def copy(src, dst, send, recv, dev):
        return pltpu.make_async_remote_copy(
            src_ref=src, dst_ref=dst, send_sem=send, recv_sem=recv,
            device_id=dev, device_id_type=MESH,
        )

    def up(i):
        if i < 2:
            src, zo = table.at[i], z
        else:
            zo = lax.rem(z - i // 2 + NZ, NZ)
            src = tabs.at[zo, i % 2]
        return copy(src, tabs.at[zo, i % 2], up_send.at[i], up_recv.at[i], above)

    def half_of(i):
        return 1 if i == 6 else i % 2

    def down(i):
        if i < 2:
            src, zo = table.at[i], z
        else:
            zo = lax.rem(z + i // 2, NZ)
            src = tabs.at[zo, half_of(i)]
        return copy(src, tabs.at[zo, half_of(i)], dn_send.at[i], dn_recv.at[i], below)

    for i in range(2):
        up(i).start()
        down(i).start()

    own_tab = pltpu.make_async_copy(table, tabs.at[z], own_sem.at[0])
    own_tab.start()
    mine = pl.ds(pl.multiple_of(n * SUB, SUB), SUB)
    here = pl.ds(pl.multiple_of(n * PART, PART), PART)
    own_samp = pltpu.make_async_copy(samples.at[:, mine], samp.at[here], own_sem.at[1])
    own_samp.start()
    s_copies = []
    for d in range(1, NN):
        there = pl.ds(pl.multiple_of(lax.rem(n + d, NN) * SUB, SUB), SUB)
        c = copy(samples.at[:, there], samp.at[here], s_send.at[d - 1], s_recv.at[d - 1], npeers[d - 1])
        c.start()
        s_copies.append(c)

    upper[...] = hot(iota((BLK, BLK), 0) < iota((BLK, BLK), 1))
    picked[...] = jnp.zeros_like(picked)
    centre[...] = jnp.zeros_like(centre)

    def prep(b, carry):
        cols = pl.ds(pl.multiple_of(b * BLK, BLK), BLK)
        a = assign[:, cols]
        near = hot(iota((512, BLK), 0) == (a >> 7))
        found = jnp.dot(lut[...], near, preferred_element_type=f32)
        sel = iota((128, BLK), 0) == (a & 127)
        high = jnp.sum(jnp.where(sel, found[:128], 0.0), axis=0, keepdims=True)
        low = jnp.sum(jnp.where(sel, found[128:], 0.0), axis=0, keepdims=True)
        pos = (high * 256.0 + low).astype(i32)
        owner = pos >> 11
        slot = pos & 2047
        order = (owner & 3) * NZ + (owner >> 2)
        member = jnp.where(iota((NW, BLK), 0) == order, 1.0, 0.0)
        before = jnp.dot(member.astype(bf16), upper[...], preferred_element_type=f32) + carry
        rank = jnp.sum(member * before, axis=0, keepdims=True).astype(i32)
        codes[:, cols] = owner * CAP + rank
        parts = jnp.concatenate(
            [member * (slot >> 8).astype(f32), member * (slot & 255).astype(f32)], axis=0
        ).astype(bf16)
        picked[...] += nt(parts, hot(iota((CAP, BLK), 0) == rank))
        return carry + jnp.sum(member, axis=1, keepdims=True)

    lax.fori_loop(0, ROWS // BLK, prep, jnp.zeros((NW, 1), f32))
    slots = (picked[:NW] * 256.0 + picked[NW:]).astype(i32)
    for d in range(NX):
        req[d] = slots[d * NZ : (d + 1) * NZ]
    q_copies = []
    for d in range(1, NX):
        xx = lax.rem(x + d, NX)
        c = copy(req.at[xx], reqin.at[x], q_send.at[d - 1], q_recv.at[d - 1], xpeers[d - 1])
        c.start()
        q_copies.append(c)
    reqin[x] = req[x]
    own_tab.wait()
    for c in q_copies:
        c.wait()

    def give(j, d):
        return copy(
            gs.at[j, d - 1], gin.at[j, x], g_send.at[j, d - 1], g_recv.at[j, d - 1],
            {"wide": z * NX + lax.rem(x + d, NX)},
        )

    def table_of(j):
        step = (j + 1) // 2
        return lax.rem(z + step * (1 - 2 * lax.rem(j, 2)) + NZ, NZ)

    def gather(j):
        zo = table_of(j)

        def rows_for(d):
            xx = lax.rem(x + d, NX)
            want = reqin[xx, pl.ds(zo, 1), :]
            got = jnp.zeros((SUB, CAP), f32)
            for h in range(2):
                pick = hot(iota((K // 2, CAP), 0) + h * (K // 2) == want)
                got = got + jnp.dot(tabs[zo, h], pick, preferred_element_type=f32)
            return got.astype(bf16)

        def one(d, _):
            gs[j, d - 1] = rows_for(d)
            give(j, d).start()
            return 0

        lax.fori_loop(1, NX, one, 0)
        gin[j, x] = rows_for(0)

    def consume(j):
        zo = table_of(j)

        def arrived(d, _):
            give(j, d).wait_recv()
            return 0

        lax.fori_loop(1, NX, arrived, 0)
        rows = jnp.concatenate([gin[j, d] for d in range(NX)], axis=1)

        def place(b, _):
            cols = pl.ds(pl.multiple_of(b * BLK, BLK), BLK)
            where = codes[:, cols] - zo * (NX * CAP)
            spot = hot(iota((NX * CAP, BLK), 0) == where)
            centre[:, cols] += jnp.dot(rows, spot, preferred_element_type=f32)
            return 0

        lax.fori_loop(0, ROWS // BLK, place, 0)

    due = {1: (0, 1), 2: (2,), 3: (3,), 4: (4,), 5: (5,), 7: (6,)}

    def forward(i):
        up(i).wait_recv()
        if i + 2 <= 6:
            up(i + 2).start()
        down(i).wait_recv()
        if i == 5:
            down(6).start()
        elif i + 2 <= 5:
            down(i + 2).start()

    def step(j, _):
        for when, which in due.items():
            @pl.when(j == when)
            def _():
                for i in which:
                    forward(i)

        gather(j)

        @pl.when(j > 0)
        def _():
            consume(j - 1)

        return 0

    lax.fori_loop(0, NZ, step, 0)
    consume(NZ - 1)
    own_samp.wait()
    for c in s_copies:
        c.wait()

    def finish(b, _):
        at = pl.ds(pl.multiple_of(b * BLK, BLK), BLK)
        mid = centre[:, at].T
        out[at, :] = (samp[at, :].astype(f32) - mid).astype(bf16)
        return 0

    lax.fori_loop(0, ROWS // BLK, finish, 0)
    for i in range(7):
        up(i).wait_send()
        down(i).wait_send()

    def sent(k, _):
        give(k // 3, lax.rem(k, 3) + 1).wait_send()
        return 0

    lax.fori_loop(0, NZ * 3, sent, 0)


RB = 256
SCALE = math.log2(math.e) / 8.0


def em_kernel(
    rows, book, out,
    aug, scaled, words, probs, score,
    xs, xc, xin, xcin, zs, zc, zin, zcin, fresh, norm, normz, normx, own,
    x_send, x_recv, xc_send, xc_recv, z_send, z_recv, zc_send, zc_recv,
    az_send, az_recv, an_send, an_recv, ax_send, ax_recv, am_send, am_recv,
):
    w = lax.axis_index("wide")
    z = w // NX
    x = lax.rem(w, NX)
    xpeers = [{"wide": z * NX + lax.rem(x + d, NX)} for d in range(1, NX)]
    zpeers = [{"wide": lax.rem(z + d, NZ) * NX + x} for d in range(1, NZ)]
    greet(xpeers + zpeers)

    def copy(src, dst, send, recv, dev):
        return pltpu.make_async_remote_copy(
            src_ref=src, dst_ref=dst, send_sem=send, recv_sem=recv,
            device_id=dev, device_id_type=MESH,
        )

    lane = iota((1, SUB), 1)

    def extra(half):
        hi = half.astype(bf16).astype(f32)
        mid = (half - hi).astype(bf16).astype(f32)
        lo = half - hi - mid
        return jnp.where(lane == 0, hi, jnp.where(lane == 1, mid, jnp.where(lane == 2, lo, 0.0)))

    aug[:, :SUB] = rows[...]
    aug[:, SUB:] = jnp.broadcast_to(jnp.where(lane < 3, 1.0, 0.0), (ROWS, SUB)).astype(bf16)

    def load(b, _):
        at = pl.ds(pl.multiple_of(b * 256, 256), 256)
        c = book[at, :]
        words[at, :SUB] = c.astype(bf16)
        words[at, SUB:] = extra(-0.5 * jnp.sum(c * c, axis=1, keepdims=True)).astype(bf16)
        return 0

    lax.fori_loop(0, K // 256, load, 0)
    base = pl.multiple_of(x * XK, XK)
    first = pl.multiple_of(base + z * OWN, OWN)
    own[...] = book[pl.ds(first, OWN), :]
    pending = []

    for it in range(ITERS):
        def block(b, _):
            at = pl.ds(pl.multiple_of(b * RB, RB), RB)
            r = aug[at, :]
            score[...] = nt(words[...], r)
            top = jnp.max(score[...], axis=0, keepdims=True)
            p = jnp.exp2((score[...] - top) * SCALE)
            probs[:, at] = p.astype(bf16)
            inv = 1.0 / jnp.sum(p, axis=0, keepdims=True)
            invt = jnp.broadcast_to(inv, (SUB, RB)).T
            scaled[at, :SUB] = (r[:, :SUB].astype(f32) * invt).astype(bf16)
            hi = invt.astype(bf16).astype(f32)
            scaled[at, SUB:] = jnp.where(lane == 0, hi, jnp.where(lane == 1, invt - hi, 0.0)).astype(bf16)
            return 0

        lax.fori_loop(0, ROWS // RB, block, 0)

        def chunk(xx):
            at = pl.ds(pl.multiple_of(xx * XK, XK), XK)
            t = jnp.dot(probs[at, :], scaled[...], preferred_element_type=f32)
            c = t[:, SUB : SUB + 1] + t[:, SUB + 1 : SUB + 2]
            spread = jnp.where(iota((XK, SUB), 1) == lax.rem(iota((XK, SUB), 0), SUB), c, 0.0)
            c = jnp.sum(spread.reshape(XK // SUB, SUB, SUB), axis=1)
            return t[:, :SUB], jnp.concatenate([c, jnp.zeros_like(c)], axis=0)

        sends = []
        for d in (2, 1, 3):
            t, c = chunk(lax.rem(x + d, NX))
            xs[it, d - 1] = t.astype(bf16)
            xc[it, d - 1] = c
            a = copy(xs.at[it, d - 1], xin.at[it, d - 1], x_send.at[it, d - 1], x_recv.at[it, d - 1], xpeers[d - 1])
            e = copy(xc.at[it, d - 1], xcin.at[it, d - 1], xc_send.at[it, d - 1], xc_recv.at[it, d - 1], xpeers[d - 1])
            a.start()
            e.start()
            sends += [a, e]
        total, count = chunk(x)
        for s in sends:
            s.wait_recv()
        for d in range(3):
            total = total + xin[it, d].astype(f32)
            count = count + xcin[it, d]
        zs[it] = total.astype(bf16)
        score[pl.ds(0, XK), :SUB] = total
        zc[it] = count
        pending += sends

        sends = []
        for d in (4, 3, 5, 2, 6, 1, 7):
            zz = lax.rem(z + d, NZ)
            a = copy(zs.at[it, pl.ds(pl.multiple_of(zz * OWN, OWN), OWN)], zin.at[it, d - 1],
                     z_send.at[it, d - 1], z_recv.at[it, d - 1], zpeers[d - 1])
            e = copy(zc.at[it], zcin.at[it, d - 1], zc_send.at[it, d - 1], zc_recv.at[it, d - 1], zpeers[d - 1])
            a.start()
            e.start()
            sends += [a, e]
        part = score[pl.ds(pl.multiple_of(z * OWN, OWN), OWN), :SUB]
        for s in sends:
            s.wait_recv()
        for d in range(NZ - 1):
            part = part + zin[it, d].astype(f32)
            count = count + zcin[it, d]
        pending += sends
        normz[...] = count
        line = normz[pl.ds(z // 2, 1), :]
        spot = iota((OWN, SUB), 1) == iota((OWN, SUB), 0) + lax.rem(z, 2) * OWN
        cnt = jnp.sum(jnp.where(spot, jnp.broadcast_to(line, (OWN, SUB)), 0.0), axis=1, keepdims=True)
        new = (part + own[...]) / (cnt + 1.0)
        own[...] = new
        fresh[it, pl.ds(first, OWN), :] = new.astype(bf16)
        last = it == ITERS - 1
        if not last:
            half = -0.5 * jnp.sum(new * new, axis=1, keepdims=True)
            flat = jnp.sum(jnp.where(spot, half, 0.0), axis=0, keepdims=True)
            norm[...] = jnp.where(iota((8, SUB), 0) == z // 2, flat, 0.0)

        sends = []
        for d in (4, 3, 5, 2, 6, 1, 7):
            src = fresh.at[it, pl.ds(first, OWN)]
            a = copy(src, src, az_send.at[it, d - 1], az_recv.at[it, d - 1], zpeers[d - 1])
            a.start()
            sends.append(a)
            if not last:
                e = copy(norm, normx.at[NX + d - 1], an_send.at[d - 1], an_recv.at[d - 1], zpeers[d - 1])
                e.start()
                sends.append(e)
        for s in sends:
            s.wait_recv()
        pending += sends
        if not last:
            mine = norm[...]
            for d in range(NZ - 1):
                mine = mine + normx[NX + d]
            normx[x] = mine
        sends = []
        for d in (2, 1, 3):
            src = fresh.at[it, pl.ds(base, XK)]
            a = copy(src, src, ax_send.at[it, d - 1], ax_recv.at[it, d - 1], xpeers[d - 1])
            a.start()
            sends.append(a)
            if not last:
                e = copy(normx.at[x], normx.at[x], am_send.at[d - 1], am_recv.at[d - 1], xpeers[d - 1])
                e.start()
                sends.append(e)
        for s in sends:
            s.wait_recv()
        pending += sends
        if last:
            out[...] = fresh[it].astype(f32)
        else:
            words[:, :SUB] = fresh[it]
            for xx in range(NX):
                for q in range(XK // SUB):
                    at = pl.ds(xx * XK + q * SUB, SUB)
                    half = jnp.broadcast_to(normx[xx, q : q + 1, :], (SUB, SUB)).T
                    words[at, SUB:] = extra(half).astype(bf16)
    for s in pending:
        s.wait_send()


def vmem():
    return pl.BlockSpec(memory_space=pltpu.VMEM)


def exchange(samples, table, lut, assign):
    dma = pltpu.SemaphoreType.DMA
    return pl.pallas_call(
        exchange_kernel,
        out_shape=jax.ShapeDtypeStruct((ROWS, SUB), bf16),
        in_specs=[pl.BlockSpec(memory_space=pl.ANY), vmem(), vmem(), vmem()],
        out_specs=vmem(),
        scratch_shapes=[
            pltpu.VMEM((ROWS, SUB), bf16),
            pltpu.VMEM((NZ, 2, SUB, K // 2), bf16),
            pltpu.VMEM((NX, NZ, CAP), i32),
            pltpu.VMEM((NX, NZ, CAP), i32),
            pltpu.VMEM((NZ, NX - 1, SUB, CAP), bf16),
            pltpu.VMEM((NZ, NX, SUB, CAP), bf16),
            pltpu.VMEM((BLK, BLK), bf16),
            pltpu.VMEM((1, ROWS), i32),
            pltpu.VMEM((2 * NW, CAP), f32),
            pltpu.VMEM((SUB, ROWS), f32),
            dma((2,)), dma((7,)), dma((7,)), dma((7,)), dma((7,)), dma((7,)), dma((7,)),
            dma((3,)), dma((3,)), dma((NZ, 3)), dma((NZ, 3)),
        ],
        compiler_params=pltpu.CompilerParams(
            collective_id=0, has_side_effects=True, vmem_limit_bytes=48 << 20
        ),
        name="exchange",
    )(samples, table, lut, assign)


def refine(rows, book):
    dma = pltpu.SemaphoreType.DMA
    x3, z7 = (ITERS, 3), (ITERS, 7)
    return pl.pallas_call(
        em_kernel,
        out_shape=jax.ShapeDtypeStruct((K, SUB), f32),
        in_specs=[vmem(), vmem()],
        out_specs=vmem(),
        scratch_shapes=[
            pltpu.VMEM((ROWS, 2 * SUB), bf16),
            pltpu.VMEM((ROWS, 2 * SUB), bf16),
            pltpu.VMEM((K, 2 * SUB), bf16),
            pltpu.VMEM((K, ROWS), bf16),
            pltpu.VMEM((K, RB), f32),
            pltpu.VMEM((ITERS, 3, XK, SUB), bf16),
            pltpu.VMEM((ITERS, 3, 8, SUB), f32),
            pltpu.VMEM((ITERS, 3, XK, SUB), bf16),
            pltpu.VMEM((ITERS, 3, 8, SUB), f32),
            pltpu.VMEM((ITERS, XK, SUB), bf16),
            pltpu.VMEM((ITERS, 8, SUB), f32),
            pltpu.VMEM((ITERS, 7, OWN, SUB), bf16),
            pltpu.VMEM((ITERS, 7, 8, SUB), f32),
            pltpu.VMEM((ITERS, K, SUB), bf16),
            pltpu.VMEM((8, SUB), f32),
            pltpu.VMEM((8, SUB), f32),
            pltpu.VMEM((NX + 7, 8, SUB), f32),
            pltpu.VMEM((OWN, SUB), f32),
            dma(x3), dma(x3), dma(x3), dma(x3), dma(z7), dma(z7), dma(z7), dma(z7),
            dma(z7), dma(z7), dma((7,)), dma((7,)), dma(x3), dma(x3), dma((3,)), dma((3,)),
        ],
        compiler_params=pltpu.CompilerParams(
            collective_id=1, has_side_effects=True, vmem_limit_bytes=56 << 20
        ),
        name="refine",
    )(rows, book)


def on_device(samples, centroid_table, owner, slot, assign, codebook):
    pos = (owner * K + slot).reshape(512, 128)
    lut = jnp.concatenate([(pos >> 8).T, (pos & 255).T], axis=0).astype(bf16)
    table = centroid_table.reshape(2, K // 2, SUB).transpose(0, 2, 1)
    residual = exchange(samples, table, lut, assign.reshape(1, ROWS))
    refined = refine(residual, codebook[0])
    return residual, refined[None]


def solution(mesh):
    return jax.shard_map(
        on_device,
        mesh=mesh,
        in_specs=(
            P(("wide", "narrow"), None),
            P("wide", "narrow"),
            P(),
            P(),
            P("wide"),
            P("narrow", None, None),
        ),
        out_specs=(P("wide", "narrow"), P("narrow", None, None)),
        check_vma=False,
    )
```

```python
import functools
import math

import jax
import jax.numpy as jnp
from jax import lax
from jax.experimental import pallas as pl
from jax.experimental.pallas import tpu as pltpu
from jax.sharding import PartitionSpec as P

ITERS = 2
NZ, NX, NN = 8, 4, 8
NW = NZ * NX
CAP = 256
ROWS = 4096
K = 2048
SUB = 128
PART = 512
XK = K // NX
OWN = XK // NZ
BLK = 512
MESH = pl.DeviceIdType.MESH
f32, bf16, i32 = jnp.float32, jnp.bfloat16, jnp.int32


def iota(shape, dim):
    return lax.broadcasted_iota(i32, shape, dim)


def hot(mask):
    return jnp.where(mask, 1.0, 0.0).astype(bf16)


def nt(a, b):
    return lax.dot_general(a, b, (((1,), (1,)), ((), ())), preferred_element_type=f32)


def greet(peers):
    barrier = pltpu.get_barrier_semaphore()
    for peer in peers:
        pl.semaphore_signal(barrier, inc=1, device_id=peer, device_id_type=MESH)
    pl.semaphore_wait(barrier, len(peers))


def exchange_kernel(
    samples, table, lut, assign, out,
    samp, tabs, req, reqin, gs, gin, upper, codes, picked, centre,
    own_sem, s_send, s_recv, up_send, up_recv, dn_send, dn_recv,
    q_send, q_recv, g_send, g_recv,
):
    w = lax.axis_index("wide")
    n = lax.axis_index("narrow")
    z = w // NX
    x = lax.rem(w, NX)

    def at_zx(zz, xx):
        return {"wide": lax.rem(zz + NZ, NZ) * NX + lax.rem(xx + NX, NX)}

    xpeers = [at_zx(z, x + d) for d in range(1, NX)]
    npeers = [{"narrow": lax.rem(n + d, NN)} for d in range(1, NN)]
    above, below = at_zx(z + 1, x), at_zx(z - 1, x)
    greet([above, below] + xpeers + npeers)

    def copy(src, dst, send, recv, dev):
        return pltpu.make_async_remote_copy(
            src_ref=src, dst_ref=dst, send_sem=send, recv_sem=recv,
            device_id=dev, device_id_type=MESH,
        )

    def up(i):
        if i < 2:
            src, zo = table.at[i], z
        else:
            zo = lax.rem(z - i // 2 + NZ, NZ)
            src = tabs.at[zo, i % 2]
        return copy(src, tabs.at[zo, i % 2], up_send.at[i], up_recv.at[i], above)

    def half_of(i):
        return 1 if i == 6 else i % 2

    def down(i):
        if i < 2:
            src, zo = table.at[i], z
        else:
            zo = lax.rem(z + i // 2, NZ)
            src = tabs.at[zo, half_of(i)]
        return copy(src, tabs.at[zo, half_of(i)], dn_send.at[i], dn_recv.at[i], below)

    for i in range(2):
        up(i).start()
        down(i).start()

    own_tab = pltpu.make_async_copy(table, tabs.at[z], own_sem.at[0])
    own_tab.start()
    mine = pl.ds(pl.multiple_of(n * SUB, SUB), SUB)
    here = pl.ds(pl.multiple_of(n * PART, PART), PART)
    own_samp = pltpu.make_async_copy(samples.at[:, mine], samp.at[here], own_sem.at[1])
    own_samp.start()
    s_copies = []
    for d in range(1, NN):
        there = pl.ds(pl.multiple_of(lax.rem(n + d, NN) * SUB, SUB), SUB)
        c = copy(samples.at[:, there], samp.at[here], s_send.at[d - 1], s_recv.at[d - 1], npeers[d - 1])
        c.start()
        s_copies.append(c)

    upper[...] = hot(iota((BLK, BLK), 0) < iota((BLK, BLK), 1))
    picked[...] = jnp.zeros_like(picked)
    centre[...] = jnp.zeros_like(centre)

    def prep(b, carry):
        cols = pl.ds(pl.multiple_of(b * BLK, BLK), BLK)
        a = assign[:, cols]
        near = hot(iota((512, BLK), 0) == (a >> 7))
        found = jnp.dot(lut[...], near, preferred_element_type=f32)
        sel = iota((128, BLK), 0) == (a & 127)
        high = jnp.sum(jnp.where(sel, found[:128], 0.0), axis=0, keepdims=True)
        low = jnp.sum(jnp.where(sel, found[128:], 0.0), axis=0, keepdims=True)
        pos = (high * 256.0 + low).astype(i32)
        owner = pos >> 11
        slot = pos & 2047
        order = (owner & 3) * NZ + (owner >> 2)
        member = jnp.where(iota((NW, BLK), 0) == order, 1.0, 0.0)
        before = jnp.dot(member.astype(bf16), upper[...], preferred_element_type=f32) + carry
        rank = jnp.sum(member * before, axis=0, keepdims=True).astype(i32)
        codes[:, cols] = owner * CAP + rank
        parts = jnp.concatenate(
            [member * (slot >> 8).astype(f32), member * (slot & 255).astype(f32)], axis=0
        ).astype(bf16)
        picked[...] += nt(parts, hot(iota((CAP, BLK), 0) == rank))
        return carry + jnp.sum(member, axis=1, keepdims=True)

    lax.fori_loop(0, ROWS // BLK, prep, jnp.zeros((NW, 1), f32))
    slots = (picked[:NW] * 256.0 + picked[NW:]).astype(i32)
    for d in range(NX):
        req[d] = slots[d * NZ : (d + 1) * NZ]
    q_copies = []
    for d in range(1, NX):
        xx = lax.rem(x + d, NX)
        c = copy(req.at[xx], reqin.at[x], q_send.at[d - 1], q_recv.at[d - 1], xpeers[d - 1])
        c.start()
        q_copies.append(c)
    reqin[x] = req[x]
    own_tab.wait()
    for c in q_copies:
        c.wait()

    def give(j, d):
        return copy(
            gs.at[j, d - 1], gin.at[j, x], g_send.at[j, d - 1], g_recv.at[j, d - 1],
            {"wide": z * NX + lax.rem(x + d, NX)},
        )

    def table_of(j):
        step = (j + 1) // 2
        return lax.rem(z + step * (1 - 2 * lax.rem(j, 2)) + NZ, NZ)

    def gather(j):
        zo = table_of(j)

        def rows_for(d):
            xx = lax.rem(x + d, NX)
            want = reqin[xx, pl.ds(zo, 1), :]
            got = jnp.zeros((SUB, CAP), f32)
            for h in range(2):
                pick = hot(iota((K // 2, CAP), 0) + h * (K // 2) == want)
                got = got + jnp.dot(tabs[zo, h], pick, preferred_element_type=f32)
            return got.astype(bf16)

        def one(e, _):
            d = lax.rem(e + 1, NX - 1) + 1
            gs[j, d - 1] = rows_for(d)
            give(j, d).start()
            return 0

        lax.fori_loop(0, NX - 1, one, 0)
        gin[j, x] = rows_for(0)

    def consume(j, last=False):
        zo = table_of(j)

        def arrived(d, _):
            give(j, d).wait_recv()
            return 0

        lax.fori_loop(1, NX, arrived, 0)
        rows = jnp.concatenate([gin[j, d] for d in range(NX)], axis=1)

        def place(b, _):
            cols = pl.ds(pl.multiple_of(b * BLK, BLK), BLK)
            where = codes[:, cols] - zo * (NX * CAP)
            spot = hot(iota((NX * CAP, BLK), 0) == where)
            mid = centre[:, cols] + jnp.dot(rows, spot, preferred_element_type=f32)
            if last:
                out[cols, :] = (samp[cols, :].astype(f32) - mid.T).astype(bf16)
            else:
                centre[:, cols] = mid
            return 0

        lax.fori_loop(0, ROWS // BLK, place, 0)

    due = {1: (0, 1), 2: (2,), 3: (3,), 4: (4,), 5: (5,), 7: (6,)}

    def forward(i):
        up(i).wait_recv()
        if i + 2 <= 6:
            up(i + 2).start()
        down(i).wait_recv()
        if i == 5:
            down(6).start()
        elif i + 2 <= 5:
            down(i + 2).start()

    def step(j, _):
        for when, which in due.items():
            @pl.when(j == when)
            def _():
                for i in which:
                    forward(i)

        gather(j)

        @pl.when(j == NZ - 1)
        def _():
            consume(NZ - 3)

        @pl.when(j > 0)
        def _():
            @pl.when(j != NZ - 2)
            def _():
                consume(j - 1)

        return 0

    lax.fori_loop(0, NZ, step, 0)
    own_samp.wait()
    for c in s_copies:
        c.wait()
    consume(NZ - 1, last=True)
    for i in range(7):
        up(i).wait_send()
        down(i).wait_send()

    def sent(k, _):
        give(k // 3, lax.rem(k, 3) + 1).wait_send()
        return 0

    lax.fori_loop(0, NZ * 3, sent, 0)


RB = 512
KC = 256
XH = XK // 2
SCALE = math.log2(math.e) / 8.0


def em_kernel(
    rows, book, out,
    aug, scaled, words, probs, score, score2,
    xs, keep, xc, xin, xcin, zs, zc, zin, zcin, fresh, norm, normz, normx, own,
    x_send, x_recv, xc_send, xc_recv, z_send, z_recv, zc_send, zc_recv,
    az_send, az_recv, an_send, an_recv, ax_send, ax_recv, am_send, am_recv,
):
    w = lax.axis_index("wide")
    z = w // NX
    x = lax.rem(w, NX)
    xpeers = [{"wide": z * NX + lax.rem(x + d, NX)} for d in range(1, NX)]
    zpeers = [{"wide": lax.rem(z + d, NZ) * NX + x} for d in range(1, NZ)]
    greet(xpeers + zpeers)

    def copy(src, dst, send, recv, dev):
        return pltpu.make_async_remote_copy(
            src_ref=src, dst_ref=dst, send_sem=send, recv_sem=recv,
            device_id=dev, device_id_type=MESH,
        )

    lane = iota((1, SUB), 1)

    def extra(half):
        hi = half.astype(bf16).astype(f32)
        mid = (half - hi).astype(bf16).astype(f32)
        lo = half - hi - mid
        return jnp.where(lane == 0, hi, jnp.where(lane == 1, mid, jnp.where(lane == 2, lo, 0.0)))

    aug[:, :SUB] = rows[...]
    aug[:, SUB:] = jnp.broadcast_to(jnp.where(lane < 3, 1.0, 0.0), (ROWS, SUB)).astype(bf16)

    def load(b, _):
        at = pl.ds(pl.multiple_of(b * 256, 256), 256)
        c = book[at, :]
        words[at, :SUB] = c.astype(bf16)
        words[at, SUB:] = extra(-0.5 * jnp.sum(c * c, axis=1, keepdims=True)).astype(bf16)
        return 0

    lax.fori_loop(0, K // 256, load, 0)
    base = pl.multiple_of(x * XK, XK)
    first = pl.multiple_of(base + z * OWN, OWN)
    own[...] = book[pl.ds(first, OWN), :]
    pending = []

    for it in range(ITERS):
        def rows_at(b):
            return pl.ds(pl.multiple_of(b * RB, RB), RB)

        def products(k, r, dst, top):
            s = nt(words[k : k + KC, :], r)
            dst[k : k + KC, :] = s
            m = jnp.max(s.reshape(KC // 8, 8, RB), axis=0)
            return m if top is None else jnp.maximum(top, m)

        def both(nxt, dst, now, src, top):
            ahead = aug[rows_at(nxt), :]
            at = rows_at(now)
            r = aug[at, :]
            shift = jnp.max(top, axis=0, keepdims=True)
            best, mass = None, jnp.zeros((8, RB), f32)
            for k in range(0, K, KC):
                best = products(k, ahead, dst, best)
                p = jnp.exp2((src[k : k + KC, :] - shift) * SCALE)
                probs[k : k + KC, at] = p.astype(bf16)
                mass = mass + jnp.sum(p.reshape(KC // 8, 8, RB), axis=0)
            inv = 1.0 / jnp.sum(mass, axis=0, keepdims=True)
            invt = jnp.broadcast_to(inv, (SUB, RB)).T
            scaled[at, :SUB] = (r[:, :SUB].astype(f32) * invt).astype(bf16)
            hi = invt.astype(bf16).astype(f32)
            scaled[at, SUB:] = jnp.where(lane == 0, hi, jnp.where(lane == 1, invt - hi, 0.0)).astype(bf16)
            return best

        top = None
        lead = aug[pl.ds(0, RB), :]
        for k in range(0, K, KC):
            top = products(k, lead, score, top)

        def pair(i, top):
            top = both(2 * i + 1, score2, 2 * i, score, top)
            return both(lax.rem(2 * i + 2, ROWS // RB), score, 2 * i + 1, score2, top)

        lax.fori_loop(0, ROWS // RB // 2, pair, top)

        def chunk(xx):
            at = pl.ds(pl.multiple_of(xx * XK, XK), XK)
            t = jnp.dot(probs[at, :], scaled[...], preferred_element_type=f32)
            c = t[:, SUB : SUB + 1] + t[:, SUB + 1 : SUB + 2]
            spread = jnp.where(iota((XK, SUB), 1) == lax.rem(iota((XK, SUB), 0), SUB), c, 0.0)
            c = jnp.sum(spread.reshape(XK // SUB, SUB, SUB), axis=1)
            return t[:, :SUB], jnp.concatenate([c, jnp.zeros_like(c)], axis=0)

        right, across, left = xpeers

        def tell(d, c):
            xc[it, d - 1] = c
            e = copy(xc.at[it, d - 1], xcin.at[it, d - 1], xc_send.at[it, d - 1], xc_recv.at[it, d - 1], xpeers[d - 1])
            e.start()
            return e

        def part_to(q, value, dev):
            xs[it, q] = value.astype(bf16)
            a = copy(xs.at[it, q], xin.at[it, q], x_send.at[it, q], x_recv.at[it, q], dev)
            a.start()
            return a

        t, c = chunk(lax.rem(x + 2, NX))
        sends = [part_to(0, t[:XH], right), part_to(1, t[XH:], left), tell(2, c)]
        t, c = chunk(lax.rem(x + 1, NX))
        sends += [part_to(2, t[XH:], right), tell(1, c)]
        keep[:XH] = t[:XH]
        t, c = chunk(lax.rem(x + 3, NX))
        sends += [part_to(3, t[:XH], left), tell(3, c)]
        keep[XH:] = t[XH:]
        sends[0].wait_recv()
        relay = [part_to(4, keep[:XH] + xin[it, 0].astype(f32), right)]
        sends[1].wait_recv()
        relay.append(part_to(5, keep[XH:] + xin[it, 1].astype(f32), left))
        total, count = chunk(x)
        for s in sends[2:] + relay:
            s.wait_recv()
        total = total + jnp.concatenate(
            [xin[it, 4].astype(f32) + xin[it, 3].astype(f32),
             xin[it, 5].astype(f32) + xin[it, 2].astype(f32)], axis=0)
        for d in range(3):
            count = count + xcin[it, d]
        sends += relay
        zs[it] = total.astype(bf16)
        score[pl.ds(0, XK), :SUB] = total
        zc[it] = count
        pending += sends

        sends = []
        for d in (4, 3, 5, 2, 6, 1, 7):
            zz = lax.rem(z + d, NZ)
            a = copy(zs.at[it, pl.ds(pl.multiple_of(zz * OWN, OWN), OWN)], zin.at[it, d - 1],
                     z_send.at[it, d - 1], z_recv.at[it, d - 1], zpeers[d - 1])
            e = copy(zc.at[it], zcin.at[it, d - 1], zc_send.at[it, d - 1], zc_recv.at[it, d - 1], zpeers[d - 1])
            a.start()
            e.start()
            sends += [a, e]
        part = score[pl.ds(pl.multiple_of(z * OWN, OWN), OWN), :SUB]
        for s in sends:
            s.wait_recv()
        for d in range(NZ - 1):
            part = part + zin[it, d].astype(f32)
            count = count + zcin[it, d]
        pending += sends
        normz[...] = count
        line = normz[pl.ds(z // 2, 1), :]
        spot = iota((OWN, SUB), 1) == iota((OWN, SUB), 0) + lax.rem(z, 2) * OWN
        cnt = jnp.sum(jnp.where(spot, jnp.broadcast_to(line, (OWN, SUB)), 0.0), axis=1, keepdims=True)
        new = (part + own[...]) / (cnt + 1.0)
        own[...] = new
        fresh[it, pl.ds(first, OWN), :] = new.astype(bf16)
        last = it == ITERS - 1
        if not last:
            half = -0.5 * jnp.sum(new * new, axis=1, keepdims=True)
            flat = jnp.sum(jnp.where(spot, half, 0.0), axis=0, keepdims=True)
            norm[...] = jnp.where(iota((8, SUB), 0) == z // 2, flat, 0.0)

        sends = []
        for d in (4, 3, 5, 2, 6, 1, 7):
            src = fresh.at[it, pl.ds(first, OWN)]
            a = copy(src, src, az_send.at[it, d - 1], az_recv.at[it, d - 1], zpeers[d - 1])
            a.start()
            sends.append(a)
            if not last:
                e = copy(norm, normx.at[NX + d - 1], an_send.at[d - 1], an_recv.at[d - 1], zpeers[d - 1])
                e.start()
                sends.append(e)
        for s in sends:
            s.wait_recv()
        pending += sends
        if not last:
            mine = norm[...]
            for d in range(NZ - 1):
                mine = mine + normx[NX + d]
            normx[x] = mine
        def spread(q, xx, h, dev):
            src = fresh.at[it, pl.ds(pl.multiple_of(xx * XK + h * XH, XH), XH)]
            a = copy(src, src, ax_send.at[it, q], ax_recv.at[it, q], dev)
            a.start()
            return a

        sends = [spread(0, x, 0, right), spread(1, x, 1, left)]
        if not last:
            for d in (2, 1, 3):
                e = copy(normx.at[x], normx.at[x], am_send.at[d - 1], am_recv.at[d - 1], xpeers[d - 1])
                e.start()
                sends.append(e)
        sends += [spread(2, x, 1, right), spread(3, x, 0, left)]
        sends[0].wait_recv()
        relay = [spread(4, lax.rem(x + 3, NX), 0, right)]
        sends[1].wait_recv()
        relay.append(spread(5, lax.rem(x + 1, NX), 1, left))
        sends = sends + relay
        for s in sends[2:]:
            s.wait_recv()
        pending += sends
        if last:
            out[...] = fresh[it]
        else:
            words[:, :SUB] = fresh[it]
            for xx in range(NX):
                for q in range(XK // SUB):
                    at = pl.ds(xx * XK + q * SUB, SUB)
                    half = jnp.broadcast_to(normx[xx, q : q + 1, :], (SUB, SUB)).T
                    words[at, SUB:] = extra(half).astype(bf16)
    for s in pending:
        s.wait_send()


def vmem():
    return pl.BlockSpec(memory_space=pltpu.VMEM)


def exchange(samples, table, lut, assign):
    dma = pltpu.SemaphoreType.DMA
    return pl.pallas_call(
        exchange_kernel,
        out_shape=jax.ShapeDtypeStruct((ROWS, SUB), bf16),
        in_specs=[pl.BlockSpec(memory_space=pl.ANY), vmem(), vmem(), vmem()],
        out_specs=vmem(),
        scratch_shapes=[
            pltpu.VMEM((ROWS, SUB), bf16),
            pltpu.VMEM((NZ, 2, SUB, K // 2), bf16),
            pltpu.VMEM((NX, NZ, CAP), i32),
            pltpu.VMEM((NX, NZ, CAP), i32),
            pltpu.VMEM((NZ, NX - 1, SUB, CAP), bf16),
            pltpu.VMEM((NZ, NX, SUB, CAP), bf16),
            pltpu.VMEM((BLK, BLK), bf16),
            pltpu.VMEM((1, ROWS), i32),
            pltpu.VMEM((2 * NW, CAP), f32),
            pltpu.VMEM((SUB, ROWS), f32),
            dma((2,)), dma((7,)), dma((7,)), dma((7,)), dma((7,)), dma((7,)), dma((7,)),
            dma((3,)), dma((3,)), dma((NZ, 3)), dma((NZ, 3)),
        ],
        compiler_params=pltpu.CompilerParams(
            collective_id=0, has_side_effects=True, vmem_limit_bytes=48 << 20
        ),
        name="exchange",
    )(samples, table, lut, assign)


def refine(rows, book):
    dma = pltpu.SemaphoreType.DMA
    x3, z7, x6 = (ITERS, 3), (ITERS, 7), (ITERS, 6)
    return pl.pallas_call(
        em_kernel,
        out_shape=jax.ShapeDtypeStruct((K, SUB), bf16),
        in_specs=[vmem(), vmem()],
        out_specs=vmem(),
        scratch_shapes=[
            pltpu.VMEM((ROWS, 2 * SUB), bf16),
            pltpu.VMEM((ROWS, 2 * SUB), bf16),
            pltpu.VMEM((K, 2 * SUB), bf16),
            pltpu.VMEM((K, ROWS), bf16),
            pltpu.VMEM((K, RB), f32),
            pltpu.VMEM((K, RB), f32),
            pltpu.VMEM((ITERS, 6, XH, SUB), bf16),
            pltpu.VMEM((XK, SUB), f32),
            pltpu.VMEM((ITERS, 3, 8, SUB), f32),
            pltpu.VMEM((ITERS, 6, XH, SUB), bf16),
            pltpu.VMEM((ITERS, 3, 8, SUB), f32),
            pltpu.VMEM((ITERS, XK, SUB), bf16),
            pltpu.VMEM((ITERS, 8, SUB), f32),
            pltpu.VMEM((ITERS, 7, OWN, SUB), bf16),
            pltpu.VMEM((ITERS, 7, 8, SUB), f32),
            pltpu.VMEM((ITERS, K, SUB), bf16),
            pltpu.VMEM((8, SUB), f32),
            pltpu.VMEM((8, SUB), f32),
            pltpu.VMEM((NX + 7, 8, SUB), f32),
            pltpu.VMEM((OWN, SUB), f32),
            dma(x6), dma(x6), dma(x3), dma(x3), dma(z7), dma(z7), dma(z7), dma(z7),
            dma(z7), dma(z7), dma((7,)), dma((7,)), dma(x6), dma(x6), dma((3,)), dma((3,)),
        ],
        compiler_params=pltpu.CompilerParams(
            collective_id=1, has_side_effects=True, vmem_limit_bytes=56 << 20
        ),
        name="refine",
    )(rows, book)


def on_device(samples, centroid_table, owner, slot, assign, codebook):
    pos = (owner * K + slot).reshape(512, 128)
    lut = jnp.concatenate([(pos >> 8).T, (pos & 255).T], axis=0).astype(bf16)
    table = centroid_table.reshape(2, K // 2, SUB).transpose(0, 2, 1)
    residual = exchange(samples, table, lut, assign.reshape(1, ROWS))
    refined = refine(residual, codebook[0])
    return residual, refined.astype(f32)[None]


def solution(mesh):
    return jax.shard_map(
        on_device,
        mesh=mesh,
        in_specs=(
            P(("wide", "narrow"), None),
            P("wide", "narrow"),
            P(),
            P(),
            P("wide"),
            P("narrow", None, None),
        ),
        out_specs=(P("wide", "narrow"), P("narrow", None, None)),
        check_vma=False,
    )
```

```python
import functools
import math

import jax
import jax.numpy as jnp
from jax import lax
from jax.experimental import pallas as pl
from jax.experimental.pallas import tpu as pltpu
from jax.sharding import PartitionSpec as P

ITERS = 2
NZ, NX, NN = 8, 4, 8
NW = NZ * NX
CAP = 256
ROWS = 4096
K = 2048
SUB = 128
PART = 512
XK = K // NX
OWN = XK // NZ
BLK = 512
MESH = pl.DeviceIdType.MESH
f32, bf16, i32 = jnp.float32, jnp.bfloat16, jnp.int32


def iota(shape, dim):
    return lax.broadcasted_iota(i32, shape, dim)


def hot(mask):
    return jnp.where(mask, 1.0, 0.0).astype(bf16)


def nt(a, b):
    return lax.dot_general(a, b, (((1,), (1,)), ((), ())), preferred_element_type=f32)


def greet(peers):
    barrier = pltpu.get_barrier_semaphore()
    for peer in peers:
        pl.semaphore_signal(barrier, inc=1, device_id=peer, device_id_type=MESH)
    pl.semaphore_wait(barrier, len(peers))


def exchange_kernel(
    samples, table, lut, assign, out,
    samp, tabs, req, reqin, gs, gin, upper, codes, picked, centre,
    own_sem, s_send, s_recv, up_send, up_recv, dn_send, dn_recv,
    q_send, q_recv, g_send, g_recv,
):
    w = lax.axis_index("wide")
    n = lax.axis_index("narrow")
    z = w // NX
    x = lax.rem(w, NX)

    def at_zx(zz, xx):
        return {"wide": lax.rem(zz + NZ, NZ) * NX + lax.rem(xx + NX, NX)}

    xpeers = [at_zx(z, x + d) for d in range(1, NX)]
    npeers = [{"narrow": lax.rem(n + d, NN)} for d in range(1, NN)]
    above, below = at_zx(z + 1, x), at_zx(z - 1, x)
    greet([above, below] + xpeers + npeers)

    def copy(src, dst, send, recv, dev):
        return pltpu.make_async_remote_copy(
            src_ref=src, dst_ref=dst, send_sem=send, recv_sem=recv,
            device_id=dev, device_id_type=MESH,
        )

    def up(i):
        if i < 2:
            src, zo = table.at[i], z
        else:
            zo = lax.rem(z - i // 2 + NZ, NZ)
            src = tabs.at[zo, i % 2]
        return copy(src, tabs.at[zo, i % 2], up_send.at[i], up_recv.at[i], above)

    def half_of(i):
        return 1 if i == 6 else i % 2

    def down(i):
        if i < 2:
            src, zo = table.at[i], z
        else:
            zo = lax.rem(z + i // 2, NZ)
            src = tabs.at[zo, half_of(i)]
        return copy(src, tabs.at[zo, half_of(i)], dn_send.at[i], dn_recv.at[i], below)

    for i in range(2):
        up(i).start()
        down(i).start()

    own_tab = pltpu.make_async_copy(table, tabs.at[z], own_sem.at[0])
    own_tab.start()
    mine = pl.ds(pl.multiple_of(n * SUB, SUB), SUB)
    here = pl.ds(pl.multiple_of(n * PART, PART), PART)
    own_samp = pltpu.make_async_copy(samples.at[:, mine], samp.at[here], own_sem.at[1])
    own_samp.start()
    s_copies = []
    for d in range(1, NN):
        there = pl.ds(pl.multiple_of(lax.rem(n + d, NN) * SUB, SUB), SUB)
        c = copy(samples.at[:, there], samp.at[here], s_send.at[d - 1], s_recv.at[d - 1], npeers[d - 1])
        c.start()
        s_copies.append(c)

    def forward(i):
        up(i).wait_recv()
        if i + 2 <= 6:
            up(i + 2).start()
        down(i).wait_recv()
        if i == 5:
            down(6).start()
        elif i + 2 <= 5:
            down(i + 2).start()

    upper[...] = hot(iota((BLK, BLK), 0) < iota((BLK, BLK), 1))
    picked[...] = jnp.zeros_like(picked)
    centre[...] = jnp.zeros_like(centre)

    def prep(b, carry):
        cols = pl.ds(pl.multiple_of(b * BLK, BLK), BLK)
        a = assign[:, cols]
        near = hot(iota((512, BLK), 0) == (a >> 7))
        found = jnp.dot(lut[...], near, preferred_element_type=f32)
        sel = iota((128, BLK), 0) == (a & 127)
        high = jnp.sum(jnp.where(sel, found[:128], 0.0), axis=0, keepdims=True)
        low = jnp.sum(jnp.where(sel, found[128:], 0.0), axis=0, keepdims=True)
        pos = (high * 256.0 + low).astype(i32)
        owner = pos >> 11
        slot = pos & 2047
        order = (owner & 3) * NZ + (owner >> 2)
        member = jnp.where(iota((NW, BLK), 0) == order, 1.0, 0.0)
        before = jnp.dot(member.astype(bf16), upper[...], preferred_element_type=f32) + carry
        rank = jnp.sum(member * before, axis=0, keepdims=True).astype(i32)
        codes[:, cols] = owner * CAP + rank
        parts = jnp.concatenate(
            [member * (slot >> 8).astype(f32), member * (slot & 255).astype(f32)], axis=0
        ).astype(bf16)
        picked[...] += nt(parts, hot(iota((CAP, BLK), 0) == rank))
        return carry + jnp.sum(member, axis=1, keepdims=True)

    carry = lax.fori_loop(0, ROWS // BLK - 2, prep, jnp.zeros((NW, 1), f32))
    forward(0)
    lax.fori_loop(ROWS // BLK - 2, ROWS // BLK, prep, carry)
    slots = (picked[:NW] * 256.0 + picked[NW:]).astype(i32)
    for d in range(NX):
        req[d] = slots[d * NZ : (d + 1) * NZ]
    q_copies = []
    for d in range(1, NX):
        xx = lax.rem(x + d, NX)
        c = copy(req.at[xx], reqin.at[x], q_send.at[d - 1], q_recv.at[d - 1], xpeers[d - 1])
        c.start()
        q_copies.append(c)
    reqin[x] = req[x]
    own_tab.wait()
    forward(1)
    for c in q_copies:
        c.wait()

    def give(j, d):
        return copy(
            gs.at[j, d - 1], gin.at[j, x], g_send.at[j, d - 1], g_recv.at[j, d - 1],
            {"wide": z * NX + lax.rem(x + d, NX)},
        )

    def table_of(j):
        step = (j + 1) // 2
        return lax.rem(z + step * (1 - 2 * lax.rem(j, 2)) + NZ, NZ)

    def gather(j):
        zo = table_of(j)

        def rows_for(d):
            xx = lax.rem(x + d, NX)
            want = reqin[xx, pl.ds(zo, 1), :]
            got = jnp.zeros((SUB, CAP), f32)
            for h in range(2):
                pick = hot(iota((K // 2, CAP), 0) + h * (K // 2) == want)
                got = got + jnp.dot(tabs[zo, h], pick, preferred_element_type=f32)
            return got.astype(bf16)

        def one(e, _):
            d = lax.rem(e + 1, NX - 1) + 1
            gs[j, d - 1] = rows_for(d)
            give(j, d).start()
            return 0

        lax.fori_loop(0, NX - 1, one, 0)
        gin[j, x] = rows_for(0)

    def consume(j, last=False):
        zo = table_of(j)

        def arrived(d, _):
            give(j, d).wait_recv()
            return 0

        lax.fori_loop(1, NX, arrived, 0)
        rows = jnp.concatenate([gin[j, d] for d in range(NX)], axis=1)

        def place(b, _):
            cols = pl.ds(pl.multiple_of(b * BLK, BLK), BLK)
            where = codes[:, cols] - zo * (NX * CAP)
            spot = hot(iota((NX * CAP, BLK), 0) == where)
            mid = centre[:, cols] + jnp.dot(rows, spot, preferred_element_type=f32)
            if last:
                out[cols, :] = (samp[cols, :].astype(f32) - mid.T).astype(bf16)
            else:
                centre[:, cols] = mid
            return 0

        lax.fori_loop(0, ROWS // BLK, place, 0)

    due = {2: 2, 3: 3, 4: 4, 5: 5, 7: 6}

    def step(j, _):
        for when, which in due.items():
            @pl.when(j == when)
            def _():
                forward(which)

        gather(j)

        @pl.when(j == NZ - 1)
        def _():
            consume(NZ - 3)

        @pl.when(j > 0)
        def _():
            @pl.when(j != NZ - 2)
            def _():
                consume(j - 1)

        return 0

    lax.fori_loop(0, NZ, step, 0)
    own_samp.wait()
    for c in s_copies:
        c.wait()
    consume(NZ - 1, last=True)
    for i in range(7):
        up(i).wait_send()
        down(i).wait_send()

    def sent(k, _):
        give(k // 3, lax.rem(k, 3) + 1).wait_send()
        return 0

    lax.fori_loop(0, NZ * 3, sent, 0)


RB = 512
KC = 256
XH = XK // 2
SCALE = math.log2(math.e) / 8.0


def em_kernel(
    rows, book, out,
    aug, scaled, words, probs, score, score2,
    xs, keep, xc, xin, xcin, zs, zc, zin, zcin, fresh, norm, normz, normx, own,
    x_send, x_recv, xc_send, xc_recv, z_send, z_recv, zc_send, zc_recv,
    az_send, az_recv, an_send, an_recv, ax_send, ax_recv, am_send, am_recv,
):
    w = lax.axis_index("wide")
    z = w // NX
    x = lax.rem(w, NX)
    xpeers = [{"wide": z * NX + lax.rem(x + d, NX)} for d in range(1, NX)]
    zpeers = [{"wide": lax.rem(z + d, NZ) * NX + x} for d in range(1, NZ)]
    greet(xpeers + zpeers)

    def copy(src, dst, send, recv, dev):
        return pltpu.make_async_remote_copy(
            src_ref=src, dst_ref=dst, send_sem=send, recv_sem=recv,
            device_id=dev, device_id_type=MESH,
        )

    lane = iota((1, SUB), 1)

    def extra(half):
        hi = half.astype(bf16).astype(f32)
        mid = (half - hi).astype(bf16).astype(f32)
        lo = half - hi - mid
        return jnp.where(lane == 0, hi, jnp.where(lane == 1, mid, jnp.where(lane == 2, lo, 0.0)))

    aug[:, :SUB] = rows[...]
    aug[:, SUB:] = jnp.broadcast_to(jnp.where(lane < 3, 1.0, 0.0), (ROWS, SUB)).astype(bf16)

    def load(b, _):
        at = pl.ds(pl.multiple_of(b * 256, 256), 256)
        c = book[at, :]
        words[at, :SUB] = c.astype(bf16)
        words[at, SUB:] = extra(-0.5 * jnp.sum(c * c, axis=1, keepdims=True)).astype(bf16)
        return 0

    lax.fori_loop(0, K // 256, load, 0)
    base = pl.multiple_of(x * XK, XK)
    first = pl.multiple_of(base + z * OWN, OWN)
    own[...] = book[pl.ds(first, OWN), :]
    pending = []

    for it in range(ITERS):
        def rows_at(b):
            return pl.ds(pl.multiple_of(b * RB, RB), RB)

        def products(k, r, dst, top):
            s = nt(words[k : k + KC, :], r)
            dst[k : k + KC, :] = s
            m = jnp.max(s.reshape(KC // 8, 8, RB), axis=0)
            return m if top is None else jnp.maximum(top, m)

        def both(nxt, dst, now, src, top):
            ahead = aug[rows_at(nxt), :]
            at = rows_at(now)
            r = aug[at, :]
            shift = jnp.max(top, axis=0, keepdims=True)
            best, mass = None, jnp.zeros((8, RB), f32)
            for k in range(0, K, KC):
                best = products(k, ahead, dst, best)
                p = jnp.exp2((src[k : k + KC, :] - shift) * SCALE)
                probs[k : k + KC, at] = p.astype(bf16)
                mass = mass + jnp.sum(p.reshape(KC // 8, 8, RB), axis=0)
            inv = 1.0 / jnp.sum(mass, axis=0, keepdims=True)
            invt = jnp.broadcast_to(inv, (SUB, RB)).T
            scaled[at, :SUB] = (r[:, :SUB].astype(f32) * invt).astype(bf16)
            hi = invt.astype(bf16).astype(f32)
            scaled[at, SUB:] = jnp.where(lane == 0, hi, jnp.where(lane == 1, invt - hi, 0.0)).astype(bf16)
            return best

        top = None
        lead = aug[pl.ds(0, RB), :]
        for k in range(0, K, KC):
            top = products(k, lead, score, top)

        def pair(i, top):
            top = both(2 * i + 1, score2, 2 * i, score, top)
            return both(lax.rem(2 * i + 2, ROWS // RB), score, 2 * i + 1, score2, top)

        lax.fori_loop(0, ROWS // RB // 2, pair, top)

        def chunk(xx):
            at = pl.ds(pl.multiple_of(xx * XK, XK), XK)
            t = jnp.dot(probs[at, :], scaled[...], preferred_element_type=f32)
            c = t[:, SUB : SUB + 1] + t[:, SUB + 1 : SUB + 2]
            spread = jnp.where(iota((XK, SUB), 1) == lax.rem(iota((XK, SUB), 0), SUB), c, 0.0)
            c = jnp.sum(spread.reshape(XK // SUB, SUB, SUB), axis=1)
            return t[:, :SUB], jnp.concatenate([c, jnp.zeros_like(c)], axis=0)

        right, across, left = xpeers

        def tell(d, c):
            xc[it, d - 1] = c
            e = copy(xc.at[it, d - 1], xcin.at[it, d - 1], xc_send.at[it, d - 1], xc_recv.at[it, d - 1], xpeers[d - 1])
            e.start()
            return e

        def part_to(q, value, dev):
            xs[it, q] = value.astype(bf16)
            a = copy(xs.at[it, q], xin.at[it, q], x_send.at[it, q], x_recv.at[it, q], dev)
            a.start()
            return a

        t, c = chunk(lax.rem(x + 2, NX))
        sends = [part_to(0, t[:XH], right), part_to(1, t[XH:], left), tell(2, c)]
        t, c = chunk(lax.rem(x + 1, NX))
        sends += [part_to(2, t[XH:], right), tell(1, c)]
        keep[:XH] = t[:XH]
        t, c = chunk(lax.rem(x + 3, NX))
        sends += [part_to(3, t[:XH], left), tell(3, c)]
        keep[XH:] = t[XH:]
        sends[0].wait_recv()
        relay = [part_to(4, keep[:XH] + xin[it, 0].astype(f32), right)]
        sends[1].wait_recv()
        relay.append(part_to(5, keep[XH:] + xin[it, 1].astype(f32), left))
        total, count = chunk(x)
        for s in sends[2:] + relay:
            s.wait_recv()
        total = total + jnp.concatenate(
            [xin[it, 4].astype(f32) + xin[it, 3].astype(f32),
             xin[it, 5].astype(f32) + xin[it, 2].astype(f32)], axis=0)
        for d in range(3):
            count = count + xcin[it, d]
        sends += relay
        zs[it] = total.astype(bf16)
        score[pl.ds(0, XK), :SUB] = total
        zc[it] = count
        pending += sends

        sends = []
        for d in (4, 3, 5, 2, 6, 1, 7):
            zz = lax.rem(z + d, NZ)
            a = copy(zs.at[it, pl.ds(pl.multiple_of(zz * OWN, OWN), OWN)], zin.at[it, d - 1],
                     z_send.at[it, d - 1], z_recv.at[it, d - 1], zpeers[d - 1])
            e = copy(zc.at[it], zcin.at[it, d - 1], zc_send.at[it, d - 1], zc_recv.at[it, d - 1], zpeers[d - 1])
            a.start()
            e.start()
            sends += [a, e]
        part = score[pl.ds(pl.multiple_of(z * OWN, OWN), OWN), :SUB]
        for s in sends:
            s.wait_recv()
        for d in range(NZ - 1):
            part = part + zin[it, d].astype(f32)
            count = count + zcin[it, d]
        pending += sends
        normz[...] = count
        line = normz[pl.ds(z // 2, 1), :]
        spot = iota((OWN, SUB), 1) == iota((OWN, SUB), 0) + lax.rem(z, 2) * OWN
        cnt = jnp.sum(jnp.where(spot, jnp.broadcast_to(line, (OWN, SUB)), 0.0), axis=1, keepdims=True)
        new = (part + own[...]) / (cnt + 1.0)
        own[...] = new
        fresh[it, pl.ds(first, OWN), :] = new.astype(bf16)
        last = it == ITERS - 1
        if not last:
            half = -0.5 * jnp.sum(new * new, axis=1, keepdims=True)
            flat = jnp.sum(jnp.where(spot, half, 0.0), axis=0, keepdims=True)
            norm[...] = jnp.where(iota((8, SUB), 0) == z // 2, flat, 0.0)

        def block_at(xx, d):
            zz = lax.rem(z - d + NZ, NZ)
            return fresh.at[it, pl.ds(pl.multiple_of(xx * XK + zz * OWN, OWN), OWN)]

        def spread(d, q, src, dev):
            a = copy(src, src, ax_send.at[it, d, q], ax_recv.at[it, d, q], dev)
            a.start()
            return a

        over_z, norms, over_x, relays = {}, [], {}, []
        for d in (4, 3, 5, 2, 6, 1, 7):
            src = block_at(x, 0)
            over_z[d] = copy(src, src, az_send.at[it, d - 1], az_recv.at[it, d - 1], zpeers[d - 1])
            over_z[d].start()
        if not last:
            for d in (4, 3, 5, 2, 6, 1, 7):
                e = copy(norm, normx.at[NX + d - 1], an_send.at[d - 1], an_recv.at[d - 1], zpeers[d - 1])
                e.start()
                norms.append(e)

        def relay(d):
            over_x[d][d % 2].wait_recv()
            if d % 2 == 0:
                relays.append(spread(d, 2, block_at(lax.rem(x + 3, NX), d), right))
            else:
                relays.append(spread(d, 2, block_at(lax.rem(x + 1, NX), d), left))

        order = (0, 1, 7, 2, 6, 3, 5, 4)
        for at, d in enumerate(order):
            if d:
                over_z[d].wait_recv()
            src = block_at(x, d)
            over_x[d] = (spread(d, 0, src, right), spread(d, 1, src, left))
            if at >= 3:
                relay(order[at - 3])
        if not last:
            mine = norm[...]
            for d, e in enumerate(norms):
                e.wait_recv()
            for d in range(NZ - 1):
                mine = mine + normx[NX + d]
            normx[x] = mine
            norms_x = []
            for d in (2, 1, 3):
                e = copy(normx.at[x], normx.at[x], am_send.at[d - 1], am_recv.at[d - 1], xpeers[d - 1])
                e.start()
                norms_x.append(e)
        for d in order[-3:]:
            relay(d)
        for d in order:
            over_x[d][1 - d % 2].wait_recv()
        for e in relays:
            e.wait_recv()
        pending += list(over_z.values()) + norms + relays
        for pair_of in over_x.values():
            pending += list(pair_of)
        if not last:
            for e in norms_x:
                e.wait_recv()
            pending += norms_x
        if last:
            out[...] = fresh[it]
        else:
            words[:, :SUB] = fresh[it]
            for xx in range(NX):
                for q in range(XK // SUB):
                    at = pl.ds(xx * XK + q * SUB, SUB)
                    half = jnp.broadcast_to(normx[xx, q : q + 1, :], (SUB, SUB)).T
                    words[at, SUB:] = extra(half).astype(bf16)
    for s in pending:
        s.wait_send()


def vmem():
    return pl.BlockSpec(memory_space=pltpu.VMEM)


def exchange(samples, table, lut, assign):
    dma = pltpu.SemaphoreType.DMA
    return pl.pallas_call(
        exchange_kernel,
        out_shape=jax.ShapeDtypeStruct((ROWS, SUB), bf16),
        in_specs=[pl.BlockSpec(memory_space=pl.ANY), vmem(), vmem(), vmem()],
        out_specs=vmem(),
        scratch_shapes=[
            pltpu.VMEM((ROWS, SUB), bf16),
            pltpu.VMEM((NZ, 2, SUB, K // 2), bf16),
            pltpu.VMEM((NX, NZ, CAP), i32),
            pltpu.VMEM((NX, NZ, CAP), i32),
            pltpu.VMEM((NZ, NX - 1, SUB, CAP), bf16),
            pltpu.VMEM((NZ, NX, SUB, CAP), bf16),
            pltpu.VMEM((BLK, BLK), bf16),
            pltpu.VMEM((1, ROWS), i32),
            pltpu.VMEM((2 * NW, CAP), f32),
            pltpu.VMEM((SUB, ROWS), f32),
            dma((2,)), dma((7,)), dma((7,)), dma((7,)), dma((7,)), dma((7,)), dma((7,)),
            dma((3,)), dma((3,)), dma((NZ, 3)), dma((NZ, 3)),
        ],
        compiler_params=pltpu.CompilerParams(
            collective_id=0, has_side_effects=True, vmem_limit_bytes=48 << 20
        ),
        name="exchange",
    )(samples, table, lut, assign)


def refine(rows, book):
    dma = pltpu.SemaphoreType.DMA
    x3, z7, x6 = (ITERS, 3), (ITERS, 7), (ITERS, 6)
    return pl.pallas_call(
        em_kernel,
        out_shape=jax.ShapeDtypeStruct((K, SUB), bf16),
        in_specs=[vmem(), vmem()],
        out_specs=vmem(),
        scratch_shapes=[
            pltpu.VMEM((ROWS, 2 * SUB), bf16),
            pltpu.VMEM((ROWS, 2 * SUB), bf16),
            pltpu.VMEM((K, 2 * SUB), bf16),
            pltpu.VMEM((K, ROWS), bf16),
            pltpu.VMEM((K, RB), f32),
            pltpu.VMEM((K, RB), f32),
            pltpu.VMEM((ITERS, 6, XH, SUB), bf16),
            pltpu.VMEM((XK, SUB), f32),
            pltpu.VMEM((ITERS, 3, 8, SUB), f32),
            pltpu.VMEM((ITERS, 6, XH, SUB), bf16),
            pltpu.VMEM((ITERS, 3, 8, SUB), f32),
            pltpu.VMEM((ITERS, XK, SUB), bf16),
            pltpu.VMEM((ITERS, 8, SUB), f32),
            pltpu.VMEM((ITERS, 7, OWN, SUB), bf16),
            pltpu.VMEM((ITERS, 7, 8, SUB), f32),
            pltpu.VMEM((ITERS, K, SUB), bf16),
            pltpu.VMEM((8, SUB), f32),
            pltpu.VMEM((8, SUB), f32),
            pltpu.VMEM((NX + 7, 8, SUB), f32),
            pltpu.VMEM((OWN, SUB), f32),
            dma(x6), dma(x6), dma(x3), dma(x3), dma(z7), dma(z7), dma(z7), dma(z7),
            dma(z7), dma(z7), dma((7,)), dma((7,)), dma((ITERS, NZ, 3)), dma((ITERS, NZ, 3)), dma((3,)), dma((3,)),
        ],
        compiler_params=pltpu.CompilerParams(
            collective_id=1, has_side_effects=True, vmem_limit_bytes=56 << 20
        ),
        name="refine",
    )(rows, book)


def on_device(samples, centroid_table, owner, slot, assign, codebook):
    pos = (owner * K + slot).reshape(512, 128)
    lut = jnp.concatenate([(pos >> 8).T, (pos & 255).T], axis=0).astype(bf16)
    table = centroid_table.reshape(2, K // 2, SUB).transpose(0, 2, 1)
    residual = exchange(samples, table, lut, assign.reshape(1, ROWS))
    refined = refine(residual, codebook[0])
    return residual, refined.astype(f32)[None]


def solution(mesh):
    return jax.shard_map(
        on_device,
        mesh=mesh,
        in_specs=(
            P(("wide", "narrow"), None),
            P("wide", "narrow"),
            P(),
            P(),
            P("wide"),
            P("narrow", None, None),
        ),
        out_specs=(P("wide", "narrow"), P("narrow", None, None)),
        check_vma=False,
    )
```

```python
import functools
import math

import jax
import jax.numpy as jnp
from jax import lax
from jax.experimental import pallas as pl
from jax.experimental.pallas import tpu as pltpu
from jax.sharding import PartitionSpec as P

ITERS = 2
NZ, NX, NN = 8, 4, 8
NW = NZ * NX
CAP = 256
ROWS = 4096
K = 2048
SUB = 128
PART = 512
XK = K // NX
OWN = XK // NZ
BLK = 512
MESH = pl.DeviceIdType.MESH
f32, bf16, i32 = jnp.float32, jnp.bfloat16, jnp.int32


def iota(shape, dim):
    return lax.broadcasted_iota(i32, shape, dim)


def hot(mask):
    return jnp.where(mask, 1.0, 0.0).astype(bf16)


def nt(a, b):
    return lax.dot_general(a, b, (((1,), (1,)), ((), ())), preferred_element_type=f32)


def greet(peers):
    barrier = pltpu.get_barrier_semaphore()
    for peer in peers:
        pl.semaphore_signal(barrier, inc=1, device_id=peer, device_id_type=MESH)
    pl.semaphore_wait(barrier, len(peers))


def exchange_kernel(
    samples, table, lut, assign, out,
    samp, tabs, req, reqin, gs, gin, upper, codes, picked, centre,
    own_sem, s_send, s_recv, up_send, up_recv, dn_send, dn_recv,
    q_send, q_recv, g_send, g_recv,
):
    w = lax.axis_index("wide")
    n = lax.axis_index("narrow")
    z = w // NX
    x = lax.rem(w, NX)

    def at_zx(zz, xx):
        return {"wide": lax.rem(zz + NZ, NZ) * NX + lax.rem(xx + NX, NX)}

    xpeers = [at_zx(z, x + d) for d in range(1, NX)]
    npeers = [{"narrow": lax.rem(n + d, NN)} for d in range(1, NN)]
    above, below = at_zx(z + 1, x), at_zx(z - 1, x)
    greet([above, below] + xpeers + npeers)

    def copy(src, dst, send, recv, dev):
        return pltpu.make_async_remote_copy(
            src_ref=src, dst_ref=dst, send_sem=send, recv_sem=recv,
            device_id=dev, device_id_type=MESH,
        )

    def up(i):
        if i < 2:
            src, zo = table.at[i], z
        else:
            zo = lax.rem(z - i // 2 + NZ, NZ)
            src = tabs.at[zo, i % 2]
        return copy(src, tabs.at[zo, i % 2], up_send.at[i], up_recv.at[i], above)

    def half_of(i):
        return 1 if i == 6 else i % 2

    def down(i):
        if i < 2:
            src, zo = table.at[i], z
        else:
            zo = lax.rem(z + i // 2, NZ)
            src = tabs.at[zo, half_of(i)]
        return copy(src, tabs.at[zo, half_of(i)], dn_send.at[i], dn_recv.at[i], below)

    for i in range(2):
        up(i).start()
        down(i).start()

    own_tab = pltpu.make_async_copy(table, tabs.at[z], own_sem.at[0])
    own_tab.start()
    mine = pl.ds(pl.multiple_of(n * SUB, SUB), SUB)
    here = pl.ds(pl.multiple_of(n * PART, PART), PART)
    own_samp = pltpu.make_async_copy(samples.at[:, mine], samp.at[here], own_sem.at[1])
    own_samp.start()
    s_copies = []
    for d in range(1, NN):
        there = pl.ds(pl.multiple_of(lax.rem(n + d, NN) * SUB, SUB), SUB)
        c = copy(samples.at[:, there], samp.at[here], s_send.at[d - 1], s_recv.at[d - 1], npeers[d - 1])
        c.start()
        s_copies.append(c)

    upper[...] = hot(iota((BLK, BLK), 0) < iota((BLK, BLK), 1))
    picked[...] = jnp.zeros_like(picked)
    centre[...] = jnp.zeros_like(centre)

    def prep(b, carry):
        cols = pl.ds(pl.multiple_of(b * BLK, BLK), BLK)
        a = assign[:, cols]
        near = hot(iota((512, BLK), 0) == (a >> 7))
        found = jnp.dot(lut[...], near, preferred_element_type=f32)
        sel = iota((128, BLK), 0) == (a & 127)
        high = jnp.sum(jnp.where(sel, found[:128], 0.0), axis=0, keepdims=True)
        low = jnp.sum(jnp.where(sel, found[128:], 0.0), axis=0, keepdims=True)
        pos = (high * 256.0 + low).astype(i32)
        owner = pos >> 11
        slot = pos & 2047
        order = (owner & 3) * NZ + (owner >> 2)
        member = jnp.where(iota((NW, BLK), 0) == order, 1.0, 0.0)
        before = jnp.dot(member.astype(bf16), upper[...], preferred_element_type=f32) + carry
        rank = jnp.sum(member * before, axis=0, keepdims=True).astype(i32)
        codes[:, cols] = owner * CAP + rank
        parts = jnp.concatenate(
            [member * (slot >> 8).astype(f32), member * (slot & 255).astype(f32)], axis=0
        ).astype(bf16)
        picked[...] += nt(parts, hot(iota((CAP, BLK), 0) == rank))
        return carry + jnp.sum(member, axis=1, keepdims=True)

    lax.fori_loop(0, ROWS // BLK, prep, jnp.zeros((NW, 1), f32))
    slots = (picked[:NW] * 256.0 + picked[NW:]).astype(i32)
    for d in range(NX):
        req[d] = slots[d * NZ : (d + 1) * NZ]
    q_copies = []
    for d in range(1, NX):
        xx = lax.rem(x + d, NX)
        c = copy(req.at[xx], reqin.at[x], q_send.at[d - 1], q_recv.at[d - 1], xpeers[d - 1])
        c.start()
        q_copies.append(c)
    reqin[x] = req[x]
    own_tab.wait()
    for c in q_copies:
        c.wait()

    def give(j, d):
        return copy(
            gs.at[j, d - 1], gin.at[j, x], g_send.at[j, d - 1], g_recv.at[j, d - 1],
            {"wide": z * NX + lax.rem(x + d, NX)},
        )

    def table_of(j):
        step = (j + 1) // 2
        return lax.rem(z + step * (1 - 2 * lax.rem(j, 2)) + NZ, NZ)

    def gather(j):
        zo = table_of(j)

        def rows_for(d):
            xx = lax.rem(x + d, NX)
            want = reqin[xx, pl.ds(zo, 1), :]
            got = jnp.zeros((SUB, CAP), f32)
            for h in range(2):
                pick = hot(iota((K // 2, CAP), 0) + h * (K // 2) == want)
                got = got + jnp.dot(tabs[zo, h], pick, preferred_element_type=f32)
            return got.astype(bf16)

        def one(e, _):
            d = lax.rem(e + 1, NX - 1) + 1
            gs[j, d - 1] = rows_for(d)
            give(j, d).start()
            return 0

        lax.fori_loop(0, NX - 1, one, 0)
        gin[j, x] = rows_for(0)

    def consume(j, last=False):
        zo = table_of(j)

        def arrived(d, _):
            give(j, d).wait_recv()
            return 0

        lax.fori_loop(1, NX, arrived, 0)
        rows = jnp.concatenate([gin[j, d] for d in range(NX)], axis=1)

        def place(b, _):
            cols = pl.ds(pl.multiple_of(b * BLK, BLK), BLK)
            where = codes[:, cols] - zo * (NX * CAP)
            spot = hot(iota((NX * CAP, BLK), 0) == where)
            mid = centre[:, cols] + jnp.dot(rows, spot, preferred_element_type=f32)
            if last:
                out[cols, :] = (samp[cols, :].astype(f32) - mid.T).astype(bf16)
            else:
                centre[:, cols] = mid
            return 0

        lax.fori_loop(0, ROWS // BLK, place, 0)

    due = {1: (0, 1), 2: (2,), 3: (3,), 4: (4,), 5: (5,), 7: (6,)}

    def forward(i):
        up(i).wait_recv()
        if i + 2 <= 6:
            up(i + 2).start()
        down(i).wait_recv()
        if i == 5:
            down(6).start()
        elif i + 2 <= 5:
            down(i + 2).start()

    def step(j, _):
        for when, which in due.items():
            @pl.when(j == when)
            def _():
                for i in which:
                    forward(i)

        gather(j)

        @pl.when(j == NZ - 1)
        def _():
            consume(NZ - 3)

        @pl.when(j > 0)
        def _():
            @pl.when(j != NZ - 2)
            def _():
                consume(j - 1)

        return 0

    lax.fori_loop(0, NZ, step, 0)
    own_samp.wait()
    for c in s_copies:
        c.wait()
    consume(NZ - 1, last=True)
    for i in range(7):
        up(i).wait_send()
        down(i).wait_send()

    def sent(k, _):
        give(k // 3, lax.rem(k, 3) + 1).wait_send()
        return 0

    lax.fori_loop(0, NZ * 3, sent, 0)


RB = 512
KC = 256
XH = XK // 2
TAIL = 16
BOX = OWN + TAIL
SCALE = math.log2(math.e) / 8.0


def em_kernel(
    rows, book, out,
    aug, scaled, words, probs, score, score2,
    xs, keep, xin, zs, zin, fresh, line_of, own,
    x_send, x_recv, z_send, z_recv, az_send, az_recv, ax_send, ax_recv,
):
    w = lax.axis_index("wide")
    z = w // NX
    x = lax.rem(w, NX)
    xpeers = [{"wide": z * NX + lax.rem(x + d, NX)} for d in range(1, NX)]
    zpeers = [{"wide": lax.rem(z + d, NZ) * NX + x} for d in range(1, NZ)]
    greet(xpeers + zpeers)

    def copy(src, dst, send, recv, dev):
        return pltpu.make_async_remote_copy(
            src_ref=src, dst_ref=dst, send_sem=send, recv_sem=recv,
            device_id=dev, device_id_type=MESH,
        )

    lane = iota((1, SUB), 1)

    def extra(half):
        hi = half.astype(bf16).astype(f32)
        mid = (half - hi).astype(bf16).astype(f32)
        lo = half - hi - mid
        return jnp.where(lane == 0, hi, jnp.where(lane == 1, mid, jnp.where(lane == 2, lo, 0.0)))

    aug[:, :SUB] = rows[...]
    aug[:, SUB:] = jnp.broadcast_to(jnp.where(lane < 3, 1.0, 0.0), (ROWS, SUB)).astype(bf16)

    def load(b, _):
        at = pl.ds(pl.multiple_of(b * 256, 256), 256)
        c = book[at, :]
        words[at, :SUB] = c.astype(bf16)
        words[at, SUB:] = extra(-0.5 * jnp.sum(c * c, axis=1, keepdims=True)).astype(bf16)
        return 0

    lax.fori_loop(0, K // 256, load, 0)
    base = pl.multiple_of(x * XK, XK)
    first = pl.multiple_of(base + z * OWN, OWN)
    own[...] = book[pl.ds(first, OWN), :]
    pending = []

    for it in range(ITERS):
        def rows_at(b):
            return pl.ds(pl.multiple_of(b * RB, RB), RB)

        def products(k, r, dst, top):
            s = nt(words[k : k + KC, :], r)
            dst[k : k + KC, :] = s
            m = jnp.max(s.reshape(KC // 8, 8, RB), axis=0)
            return m if top is None else jnp.maximum(top, m)

        def both(nxt, dst, now, src, top):
            ahead = aug[rows_at(nxt), :]
            at = rows_at(now)
            r = aug[at, :]
            shift = jnp.max(top, axis=0, keepdims=True)
            best, mass = None, jnp.zeros((8, RB), f32)
            for k in range(0, K, KC):
                best = products(k, ahead, dst, best)
                p = jnp.exp2((src[k : k + KC, :] - shift) * SCALE)
                probs[k : k + KC, at] = p.astype(bf16)
                mass = mass + jnp.sum(p.reshape(KC // 8, 8, RB), axis=0)
            inv = 1.0 / jnp.sum(mass, axis=0, keepdims=True)
            invt = jnp.broadcast_to(inv, (SUB, RB)).T
            scaled[at, :SUB] = (r[:, :SUB].astype(f32) * invt).astype(bf16)
            hi = invt.astype(bf16).astype(f32)
            scaled[at, SUB:] = jnp.where(lane == 0, hi, jnp.where(lane == 1, invt - hi, 0.0)).astype(bf16)
            return best

        top = None
        lead = aug[pl.ds(0, RB), :]
        for k in range(0, K, KC):
            top = products(k, lead, score, top)

        def pair(i, top):
            top = both(2 * i + 1, score2, 2 * i, score, top)
            return both(lax.rem(2 * i + 2, ROWS // RB), score, 2 * i + 1, score2, top)

        lax.fori_loop(0, ROWS // RB // 2, pair, top)

        def chunk(xx):
            at = pl.ds(pl.multiple_of(xx * XK, XK), XK)
            t = jnp.dot(probs[at, :], scaled[...], preferred_element_type=f32)
            c = t[:, SUB : SUB + 1] + t[:, SUB + 1 : SUB + 2]
            spread = jnp.where(iota((XK, SUB), 1) == lax.rem(iota((XK, SUB), 0), SUB), c, 0.0)
            c = jnp.sum(spread.reshape(XK // SUB, SUB, SUB), axis=1)
            return t[:, :SUB], c

        right, across, left = xpeers

        def tail_of(c):
            hi = c.astype(bf16).astype(f32)
            rest = jnp.zeros((TAIL - 2 * c.shape[0], SUB), f32)
            return jnp.concatenate([hi, c - hi, rest], axis=0).astype(bf16)

        def part_to(q, value, c, dev):
            xs[it, q, :XH] = value.astype(bf16)
            xs[it, q, XH:] = tail_of(c)
            a = copy(xs.at[it, q], xin.at[it, q], x_send.at[it, q], x_recv.at[it, q], dev)
            a.start()
            return a

        def got(q):
            c = xin[it, q, XH:].astype(f32)
            return xin[it, q, :XH].astype(f32), c[0:2] + c[2:4]

        t, c = chunk(lax.rem(x + 2, NX))
        sends = [part_to(0, t[:XH], c[:2], right), part_to(1, t[XH:], c[2:], left)]
        t, c = chunk(lax.rem(x + 1, NX))
        sends.append(part_to(2, t[XH:], c[2:], right))
        keep[:XH] = t[:XH]
        ahead_c = c[:2]
        t, c = chunk(lax.rem(x + 3, NX))
        sends.append(part_to(3, t[:XH], c[:2], left))
        keep[XH:] = t[XH:]
        behind_c = c[2:]
        sends[0].wait_recv()
        t, c = got(0)
        relay = [part_to(4, keep[:XH] + t, ahead_c + c, right)]
        sends[1].wait_recv()
        t, c = got(1)
        relay.append(part_to(5, keep[XH:] + t, behind_c + c, left))
        total, count = chunk(x)
        for s in sends[2:] + relay:
            s.wait_recv()
        (t4, c4), (t3, c3), (t5, c5), (t2, c2) = got(4), got(3), got(5), got(2)
        total = total + jnp.concatenate([t4 + t3, t5 + t2], axis=0)
        count = count + jnp.concatenate([c4 + c3, c5 + c2], axis=0)
        pending += sends + relay
        tail = tail_of(count)
        for zz in range(NZ):
            zs[it, zz, :OWN] = total[zz * OWN : (zz + 1) * OWN].astype(bf16)
            zs[it, zz, OWN:] = tail
        score[pl.ds(0, XK), :SUB] = total

        sends = []
        for d in (4, 3, 5, 2, 6, 1, 7):
            zz = lax.rem(z + d, NZ)
            a = copy(zs.at[it, zz], zin.at[it, d - 1], z_send.at[it, d - 1], z_recv.at[it, d - 1], zpeers[d - 1])
            a.start()
            sends.append(a)
        part = score[pl.ds(pl.multiple_of(z * OWN, OWN), OWN), :SUB]
        for s in sends:
            s.wait_recv()
        for d in range(NZ - 1):
            part = part + zin[it, d, :OWN].astype(f32)
            c = zin[it, d, OWN:].astype(f32)
            count = count + (c[0:4] + c[4:8])
        pending += sends
        line_of[...] = jnp.concatenate([count, count], axis=0)
        line = line_of[pl.ds(z // 2, 1), :]
        spot = iota((OWN, SUB), 1) == iota((OWN, SUB), 0) + lax.rem(z, 2) * OWN
        cnt = jnp.sum(jnp.where(spot, jnp.broadcast_to(line, (OWN, SUB)), 0.0), axis=1, keepdims=True)
        new = (part + own[...]) / (cnt + 1.0)
        own[...] = new
        half = -0.5 * jnp.sum(new * new, axis=1, keepdims=True)
        flat = jnp.sum(jnp.where(spot, half, 0.0), axis=0, keepdims=True)
        hi = flat.astype(bf16).astype(f32)
        mid = (flat - hi).astype(bf16).astype(f32)
        row = iota((TAIL, SUB), 0)
        fresh[it, x, z, :OWN] = new.astype(bf16)
        fresh[it, x, z, OWN:] = jnp.where(
            row == 0, hi, jnp.where(row == 1, mid, jnp.where(row == 2, flat - hi - mid, 0.0))
        ).astype(bf16)
        last = it == ITERS - 1

        sends = []
        for d in (4, 3, 5, 2, 6, 1, 7):
            src = fresh.at[it, x, z]
            a = copy(src, src, az_send.at[it, d - 1], az_recv.at[it, d - 1], zpeers[d - 1])
            a.start()
            sends.append(a)
        for s in sends:
            s.wait_recv()
        pending += sends

        def spread(q, xx, h, dev):
            src = fresh.at[it, xx, pl.ds(h * (NZ // 2), NZ // 2)]
            a = copy(src, src, ax_send.at[it, q], ax_recv.at[it, q], dev)
            a.start()
            return a

        sends = [spread(0, x, 0, right), spread(1, x, 1, left), spread(2, x, 1, right), spread(3, x, 0, left)]
        sends[0].wait_recv()
        relay = [spread(4, lax.rem(x + 3, NX), 0, right)]
        sends[1].wait_recv()
        relay.append(spread(5, lax.rem(x + 1, NX), 1, left))
        sends = sends + relay
        for s in sends[2:]:
            s.wait_recv()
        pending += sends
        for xx in range(NX):
            for q in range(XK // SUB):
                at = pl.ds(xx * XK + q * SUB, SUB)
                pair_rows = jnp.concatenate([fresh[it, xx, 2 * q, :OWN], fresh[it, xx, 2 * q + 1, :OWN]], axis=0)
                if last:
                    out[at, :] = pair_rows
                else:
                    words[at, :SUB] = pair_rows
                    c = fresh[it, xx, 2 * q, OWN:].astype(f32) + fresh[it, xx, 2 * q + 1, OWN:].astype(f32)
                    flat = c[0:1] + (c[1:2] + c[2:3])
                    words[at, SUB:] = extra(jnp.broadcast_to(flat, (SUB, SUB)).T).astype(bf16)
    for s in pending:
        s.wait_send()


def vmem():
    return pl.BlockSpec(memory_space=pltpu.VMEM)


def exchange(samples, table, lut, assign):
    dma = pltpu.SemaphoreType.DMA
    return pl.pallas_call(
        exchange_kernel,
        out_shape=jax.ShapeDtypeStruct((ROWS, SUB), bf16),
        in_specs=[pl.BlockSpec(memory_space=pl.ANY), vmem(), vmem(), vmem()],
        out_specs=vmem(),
        scratch_shapes=[
            pltpu.VMEM((ROWS, SUB), bf16),
            pltpu.VMEM((NZ, 2, SUB, K // 2), bf16),
            pltpu.VMEM((NX, NZ, CAP), i32),
            pltpu.VMEM((NX, NZ, CAP), i32),
            pltpu.VMEM((NZ, NX - 1, SUB, CAP), bf16),
            pltpu.VMEM((NZ, NX, SUB, CAP), bf16),
            pltpu.VMEM((BLK, BLK), bf16),
            pltpu.VMEM((1, ROWS), i32),
            pltpu.VMEM((2 * NW, CAP), f32),
            pltpu.VMEM((SUB, ROWS), f32),
            dma((2,)), dma((7,)), dma((7,)), dma((7,)), dma((7,)), dma((7,)), dma((7,)),
            dma((3,)), dma((3,)), dma((NZ, 3)), dma((NZ, 3)),
        ],
        compiler_params=pltpu.CompilerParams(
            collective_id=0, has_side_effects=True, vmem_limit_bytes=48 << 20
        ),
        name="exchange",
    )(samples, table, lut, assign)


def refine(rows, book):
    dma = pltpu.SemaphoreType.DMA
    z7, x6 = (ITERS, 7), (ITERS, 6)
    return pl.pallas_call(
        em_kernel,
        out_shape=jax.ShapeDtypeStruct((K, SUB), bf16),
        in_specs=[vmem(), vmem()],
        out_specs=vmem(),
        scratch_shapes=[
            pltpu.VMEM((ROWS, 2 * SUB), bf16),
            pltpu.VMEM((ROWS, 2 * SUB), bf16),
            pltpu.VMEM((K, 2 * SUB), bf16),
            pltpu.VMEM((K, ROWS), bf16),
            pltpu.VMEM((K, RB), f32),
            pltpu.VMEM((K, RB), f32),
            pltpu.VMEM((ITERS, 6, XH + TAIL, SUB), bf16),
            pltpu.VMEM((XK, SUB), f32),
            pltpu.VMEM((ITERS, 6, XH + TAIL, SUB), bf16),
            pltpu.VMEM((ITERS, NZ, BOX, SUB), bf16),
            pltpu.VMEM((ITERS, NZ - 1, BOX, SUB), bf16),
            pltpu.VMEM((ITERS, NX, NZ, BOX, SUB), bf16),
            pltpu.VMEM((8, SUB), f32),
            pltpu.VMEM((OWN, SUB), f32),
            dma(x6), dma(x6), dma(z7), dma(z7), dma(z7), dma(z7), dma(x6), dma(x6),
        ],
        compiler_params=pltpu.CompilerParams(
            collective_id=1, has_side_effects=True, vmem_limit_bytes=56 << 20
        ),
        name="refine",
    )(rows, book)


def on_device(samples, centroid_table, owner, slot, assign, codebook):
    pos = (owner * K + slot).reshape(512, 128)
    lut = jnp.concatenate([(pos >> 8).T, (pos & 255).T], axis=0).astype(bf16)
    table = centroid_table.reshape(2, K // 2, SUB).transpose(0, 2, 1)
    residual = exchange(samples, table, lut, assign.reshape(1, ROWS))
    refined = refine(residual, codebook[0])
    return residual, refined.astype(f32)[None]


def solution(mesh):
    return jax.shard_map(
        on_device,
        mesh=mesh,
        in_specs=(
            P(("wide", "narrow"), None),
            P("wide", "narrow"),
            P(),
            P(),
            P("wide"),
            P("narrow", None, None),
        ),
        out_specs=(P("wide", "narrow"), P("narrow", None, None)),
        check_vma=False,
    )
```

```python
import functools
import math

import jax
import jax.numpy as jnp
from jax import lax
from jax.experimental import pallas as pl
from jax.experimental.pallas import tpu as pltpu
from jax.sharding import PartitionSpec as P

ITERS = 2
NZ, NX, NN = 8, 4, 8
NW = NZ * NX
CAP = 256
ROWS = 4096
K = 2048
SUB = 128
PART = 512
XK = K // NX
OWN = XK // NZ
BLK = 512
MESH = pl.DeviceIdType.MESH
f32, bf16, i32 = jnp.float32, jnp.bfloat16, jnp.int32


def iota(shape, dim):
    return lax.broadcasted_iota(i32, shape, dim)


def hot(mask):
    return jnp.where(mask, 1.0, 0.0).astype(bf16)


def nt(a, b):
    return lax.dot_general(a, b, (((1,), (1,)), ((), ())), preferred_element_type=f32)


def greet(peers):
    barrier = pltpu.get_barrier_semaphore()
    for peer in peers:
        pl.semaphore_signal(barrier, inc=1, device_id=peer, device_id_type=MESH)
    return lambda: pl.semaphore_wait(barrier, len(peers))


def exchange_kernel(
    samples, table, lut, assign, out,
    samp, tabs, req, reqin, gs, gin, upper, codes, picked, centre,
    own_sem, s_send, s_recv, up_send, up_recv, dn_send, dn_recv,
    q_send, q_recv, g_send, g_recv,
):
    w = lax.axis_index("wide")
    n = lax.axis_index("narrow")
    z = w // NX
    x = lax.rem(w, NX)

    def at_zx(zz, xx):
        return {"wide": lax.rem(zz + NZ, NZ) * NX + lax.rem(xx + NX, NX)}

    xpeers = [at_zx(z, x + d) for d in range(1, NX)]
    npeers = [{"narrow": lax.rem(n + d, NN)} for d in range(1, NN)]
    above, below = at_zx(z + 1, x), at_zx(z - 1, x)
    settle = greet([above, below] + xpeers + npeers)
    upper[...] = hot(iota((BLK, BLK), 0) < iota((BLK, BLK), 1))
    picked[...] = jnp.zeros_like(picked)
    centre[...] = jnp.zeros_like(centre)
    settle()

    def copy(src, dst, send, recv, dev):
        return pltpu.make_async_remote_copy(
            src_ref=src, dst_ref=dst, send_sem=send, recv_sem=recv,
            device_id=dev, device_id_type=MESH,
        )

    def up(i):
        if i < 2:
            src, zo = table.at[i], z
        else:
            zo = lax.rem(z - i // 2 + NZ, NZ)
            src = tabs.at[zo, i % 2]
        return copy(src, tabs.at[zo, i % 2], up_send.at[i], up_recv.at[i], above)

    def half_of(i):
        return 1 if i == 6 else i % 2

    def down(i):
        if i < 2:
            src, zo = table.at[i], z
        else:
            zo = lax.rem(z + i // 2, NZ)
            src = tabs.at[zo, half_of(i)]
        return copy(src, tabs.at[zo, half_of(i)], dn_send.at[i], dn_recv.at[i], below)

    for i in range(2):
        up(i).start()
        down(i).start()

    own_tab = pltpu.make_async_copy(table, tabs.at[z], own_sem.at[0])
    own_tab.start()
    mine = pl.ds(pl.multiple_of(n * SUB, SUB), SUB)
    here = pl.ds(pl.multiple_of(n * PART, PART), PART)
    own_samp = pltpu.make_async_copy(samples.at[:, mine], samp.at[here], own_sem.at[1])
    own_samp.start()
    s_copies = []
    for d in range(1, NN):
        there = pl.ds(pl.multiple_of(lax.rem(n + d, NN) * SUB, SUB), SUB)
        c = copy(samples.at[:, there], samp.at[here], s_send.at[d - 1], s_recv.at[d - 1], npeers[d - 1])
        c.start()
        s_copies.append(c)

    def prep(b, carry):
        cols = pl.ds(pl.multiple_of(b * BLK, BLK), BLK)
        a = assign[:, cols]
        near = hot(iota((512, BLK), 0) == (a >> 7))
        found = jnp.dot(lut[...], near, preferred_element_type=f32)
        sel = iota((128, BLK), 0) == (a & 127)
        high = jnp.sum(jnp.where(sel, found[:128], 0.0), axis=0, keepdims=True)
        low = jnp.sum(jnp.where(sel, found[128:], 0.0), axis=0, keepdims=True)
        pos = (high * 256.0 + low).astype(i32)
        owner = pos >> 11
        slot = pos & 2047
        order = (owner & 3) * NZ + (owner >> 2)
        member = jnp.where(iota((NW, BLK), 0) == order, 1.0, 0.0)
        before = jnp.dot(member.astype(bf16), upper[...], preferred_element_type=f32) + carry
        rank = jnp.sum(member * before, axis=0, keepdims=True).astype(i32)
        codes[:, cols] = owner * CAP + rank
        parts = jnp.concatenate(
            [member * (slot >> 8).astype(f32), member * (slot & 255).astype(f32)], axis=0
        ).astype(bf16)
        picked[...] += nt(parts, hot(iota((CAP, BLK), 0) == rank))
        return carry + jnp.sum(member, axis=1, keepdims=True)

    lax.fori_loop(0, ROWS // BLK, prep, jnp.zeros((NW, 1), f32))
    slots = (picked[:NW] * 256.0 + picked[NW:]).astype(i32)
    for d in range(NX):
        req[d] = slots[d * NZ : (d + 1) * NZ]
    q_copies = []
    for d in range(1, NX):
        xx = lax.rem(x + d, NX)
        c = copy(req.at[xx], reqin.at[x], q_send.at[d - 1], q_recv.at[d - 1], xpeers[d - 1])
        c.start()
        q_copies.append(c)
    reqin[x] = req[x]
    own_tab.wait()
    for c in q_copies:
        c.wait()

    def give(j, d):
        return copy(
            gs.at[j, d - 1], gin.at[j, x], g_send.at[j, d - 1], g_recv.at[j, d - 1],
            {"wide": z * NX + lax.rem(x + d, NX)},
        )

    def table_of(j):
        step = (j + 1) // 2
        return lax.rem(z + step * (1 - 2 * lax.rem(j, 2)) + NZ, NZ)

    def gather(j):
        zo = table_of(j)

        def rows_for(d):
            xx = lax.rem(x + d, NX)
            want = reqin[xx, pl.ds(zo, 1), :]
            got = jnp.zeros((SUB, CAP), f32)
            for h in range(2):
                pick = hot(iota((K // 2, CAP), 0) + h * (K // 2) == want)
                got = got + jnp.dot(tabs[zo, h], pick, preferred_element_type=f32)
            return got.astype(bf16)

        def one(e, _):
            d = lax.rem(e + 1, NX - 1) + 1
            gs[j, d - 1] = rows_for(d)
            give(j, d).start()
            return 0

        lax.fori_loop(0, NX - 1, one, 0)
        gin[j, x] = rows_for(0)

    def consume(j, last=False):
        zo = table_of(j)

        def arrived(d, _):
            give(j, d).wait_recv()
            return 0

        lax.fori_loop(1, NX, arrived, 0)
        rows = jnp.concatenate([gin[j, d] for d in range(NX)], axis=1)

        def place(b, _):
            cols = pl.ds(pl.multiple_of(b * BLK, BLK), BLK)
            where = codes[:, cols] - zo * (NX * CAP)
            spot = hot(iota((NX * CAP, BLK), 0) == where)
            mid = centre[:, cols] + jnp.dot(rows, spot, preferred_element_type=f32)
            if last:
                out[cols, :] = (samp[cols, :].astype(f32) - mid.T).astype(bf16)
            else:
                centre[:, cols] = mid
            return 0

        lax.fori_loop(0, ROWS // BLK, place, 0)

    due = {1: (0, 1), 2: (2,), 3: (3,), 4: (4,), 5: (5,), 7: (6,)}

    def forward(i):
        up(i).wait_recv()
        if i + 2 <= 6:
            up(i + 2).start()
        down(i).wait_recv()
        if i == 5:
            down(6).start()
        elif i + 2 <= 5:
            down(i + 2).start()

    def step(j, _):
        for when, which in due.items():
            @pl.when(j == when)
            def _():
                for i in which:
                    forward(i)

        gather(j)

        @pl.when(j == NZ - 1)
        def _():
            consume(NZ - 3)

        @pl.when(j > 0)
        def _():
            @pl.when(j != NZ - 2)
            def _():
                consume(j - 1)

        return 0

    lax.fori_loop(0, NZ, step, 0)
    own_samp.wait()
    for c in s_copies:
        c.wait()
    consume(NZ - 1, last=True)
    for i in range(7):
        up(i).wait_send()
        down(i).wait_send()

    def sent(k, _):
        give(k // 3, lax.rem(k, 3) + 1).wait_send()
        return 0

    lax.fori_loop(0, NZ * 3, sent, 0)


RB = 512
KC = 256
XH = XK // 2
SCALE = math.log2(math.e) / 8.0


def em_kernel(
    rows, book, out,
    aug, scaled, words, probs, score, score2,
    xs, keep, xc, xin, xcin, zs, zc, zin, zcin, fresh, norm, normz, normx, own,
    x_send, x_recv, xc_send, xc_recv, z_send, z_recv, zc_send, zc_recv,
    az_send, az_recv, an_send, an_recv, ax_send, ax_recv, am_send, am_recv,
):
    w = lax.axis_index("wide")
    z = w // NX
    x = lax.rem(w, NX)
    xpeers = [{"wide": z * NX + lax.rem(x + d, NX)} for d in range(1, NX)]
    zpeers = [{"wide": lax.rem(z + d, NZ) * NX + x} for d in range(1, NZ)]
    settle = greet(xpeers + zpeers)

    def copy(src, dst, send, recv, dev):
        return pltpu.make_async_remote_copy(
            src_ref=src, dst_ref=dst, send_sem=send, recv_sem=recv,
            device_id=dev, device_id_type=MESH,
        )

    lane = iota((1, SUB), 1)

    def extra(half):
        hi = half.astype(bf16).astype(f32)
        mid = (half - hi).astype(bf16).astype(f32)
        lo = half - hi - mid
        return jnp.where(lane == 0, hi, jnp.where(lane == 1, mid, jnp.where(lane == 2, lo, 0.0)))

    aug[:, :SUB] = rows[...]
    aug[:, SUB:] = jnp.broadcast_to(jnp.where(lane < 3, 1.0, 0.0), (ROWS, SUB)).astype(bf16)

    def load(b, _):
        at = pl.ds(pl.multiple_of(b * 256, 256), 256)
        c = book[at, :]
        words[at, :SUB] = c.astype(bf16)
        words[at, SUB:] = extra(-0.5 * jnp.sum(c * c, axis=1, keepdims=True)).astype(bf16)
        return 0

    lax.fori_loop(0, K // 256, load, 0)
    base = pl.multiple_of(x * XK, XK)
    first = pl.multiple_of(base + z * OWN, OWN)
    own[...] = book[pl.ds(first, OWN), :]
    pending = []

    for it in range(ITERS):
        def rows_at(b):
            return pl.ds(pl.multiple_of(b * RB, RB), RB)

        def products(k, r, dst, top):
            s = nt(words[k : k + KC, :], r)
            dst[k : k + KC, :] = s
            m = jnp.max(s.reshape(KC // 8, 8, RB), axis=0)
            return m if top is None else jnp.maximum(top, m)

        def both(nxt, dst, now, src, top):
            ahead = aug[rows_at(nxt), :]
            at = rows_at(now)
            r = aug[at, :]
            shift = jnp.max(top, axis=0, keepdims=True)
            best, mass = None, jnp.zeros((8, RB), f32)
            for k in range(0, K, KC):
                best = products(k, ahead, dst, best)
                p = jnp.exp2((src[k : k + KC, :] - shift) * SCALE)
                probs[k : k + KC, at] = p.astype(bf16)
                mass = mass + jnp.sum(p.reshape(KC // 8, 8, RB), axis=0)
            inv = 1.0 / jnp.sum(mass, axis=0, keepdims=True)
            invt = jnp.broadcast_to(inv, (SUB, RB)).T
            scaled[at, :SUB] = (r[:, :SUB].astype(f32) * invt).astype(bf16)
            hi = invt.astype(bf16).astype(f32)
            scaled[at, SUB:] = jnp.where(lane == 0, hi, jnp.where(lane == 1, invt - hi, 0.0)).astype(bf16)
            return best

        top = None
        lead = aug[pl.ds(0, RB), :]
        for k in range(0, K, KC):
            top = products(k, lead, score, top)

        def pair(i, top):
            top = both(2 * i + 1, score2, 2 * i, score, top)
            return both(lax.rem(2 * i + 2, ROWS // RB), score, 2 * i + 1, score2, top)

        lax.fori_loop(0, ROWS // RB // 2, pair, top)

        def chunk(xx):
            at = pl.ds(pl.multiple_of(xx * XK, XK), XK)
            t = jnp.dot(probs[at, :], scaled[...], preferred_element_type=f32)
            c = t[:, SUB : SUB + 1] + t[:, SUB + 1 : SUB + 2]
            spread = jnp.where(iota((XK, SUB), 1) == lax.rem(iota((XK, SUB), 0), SUB), c, 0.0)
            c = jnp.sum(spread.reshape(XK // SUB, SUB, SUB), axis=1)
            return t[:, :SUB], jnp.concatenate([c, jnp.zeros_like(c)], axis=0)

        right, across, left = xpeers

        def tell(d, c):
            xc[it, d - 1] = c
            e = copy(xc.at[it, d - 1], xcin.at[it, d - 1], xc_send.at[it, d - 1], xc_recv.at[it, d - 1], xpeers[d - 1])
            e.start()
            return e

        def part_to(q, value, dev):
            xs[it, q] = value.astype(bf16)
            a = copy(xs.at[it, q], xin.at[it, q], x_send.at[it, q], x_recv.at[it, q], dev)
            a.start()
            return a

        t, c = chunk(lax.rem(x + 2, NX))
        if it == 0:
            settle()
        sends = [part_to(0, t[:XH], right), part_to(1, t[XH:], left), tell(2, c)]
        t, c = chunk(lax.rem(x + 1, NX))
        sends += [part_to(2, t[XH:], right), tell(1, c)]
        keep[:XH] = t[:XH]
        t, c = chunk(lax.rem(x + 3, NX))
        sends += [part_to(3, t[:XH], left), tell(3, c)]
        keep[XH:] = t[XH:]
        sends[0].wait_recv()
        relay = [part_to(4, keep[:XH] + xin[it, 0].astype(f32), right)]
        sends[1].wait_recv()
        relay.append(part_to(5, keep[XH:] + xin[it, 1].astype(f32), left))
        total, count = chunk(x)
        for s in sends[2:] + relay:
            s.wait_recv()
        total = total + jnp.concatenate(
            [xin[it, 4].astype(f32) + xin[it, 3].astype(f32),
             xin[it, 5].astype(f32) + xin[it, 2].astype(f32)], axis=0)
        for d in range(3):
            count = count + xcin[it, d]
        sends += relay
        zs[it] = total.astype(bf16)
        score[pl.ds(0, XK), :SUB] = total
        zc[it] = count
        pending += sends

        sends = []
        for d in (4, 3, 5, 2, 6, 1, 7):
            zz = lax.rem(z + d, NZ)
            a = copy(zs.at[it, pl.ds(pl.multiple_of(zz * OWN, OWN), OWN)], zin.at[it, d - 1],
                     z_send.at[it, d - 1], z_recv.at[it, d - 1], zpeers[d - 1])
            e = copy(zc.at[it], zcin.at[it, d - 1], zc_send.at[it, d - 1], zc_recv.at[it, d - 1], zpeers[d - 1])
            a.start()
            e.start()
            sends += [a, e]
        part = score[pl.ds(pl.multiple_of(z * OWN, OWN), OWN), :SUB]
        for s in sends:
            s.wait_recv()
        for d in range(NZ - 1):
            part = part + zin[it, d].astype(f32)
            count = count + zcin[it, d]
        pending += sends
        normz[...] = count
        line = normz[pl.ds(z // 2, 1), :]
        spot = iota((OWN, SUB), 1) == iota((OWN, SUB), 0) + lax.rem(z, 2) * OWN
        cnt = jnp.sum(jnp.where(spot, jnp.broadcast_to(line, (OWN, SUB)), 0.0), axis=1, keepdims=True)
        new = (part + own[...]) / (cnt + 1.0)
        own[...] = new
        fresh[it, pl.ds(first, OWN), :] = new.astype(bf16)
        last = it == ITERS - 1
        if not last:
            half = -0.5 * jnp.sum(new * new, axis=1, keepdims=True)
            flat = jnp.sum(jnp.where(spot, half, 0.0), axis=0, keepdims=True)
            norm[...] = jnp.where(iota((8, SUB), 0) == z // 2, flat, 0.0)

        sends = []
        for d in (4, 3, 5, 2, 6, 1, 7):
            src = fresh.at[it, pl.ds(first, OWN)]
            a = copy(src, src, az_send.at[it, d - 1], az_recv.at[it, d - 1], zpeers[d - 1])
            a.start()
            sends.append(a)
            if not last:
                e = copy(norm, normx.at[NX + d - 1], an_send.at[d - 1], an_recv.at[d - 1], zpeers[d - 1])
                e.start()
                sends.append(e)
        for s in sends:
            s.wait_recv()
        pending += sends
        if not last:
            mine = norm[...]
            for d in range(NZ - 1):
                mine = mine + normx[NX + d]
            normx[x] = mine
        def spread(q, xx, h, dev):
            src = fresh.at[it, pl.ds(pl.multiple_of(xx * XK + h * XH, XH), XH)]
            a = copy(src, src, ax_send.at[it, q], ax_recv.at[it, q], dev)
            a.start()
            return a

        sends = [spread(0, x, 0, right), spread(1, x, 1, left)]
        if not last:
            for d in (2, 1, 3):
                e = copy(normx.at[x], normx.at[x], am_send.at[d - 1], am_recv.at[d - 1], xpeers[d - 1])
                e.start()
                sends.append(e)
        sends += [spread(2, x, 1, right), spread(3, x, 0, left)]
        sends[0].wait_recv()
        relay = [spread(4, lax.rem(x + 3, NX), 0, right)]
        sends[1].wait_recv()
        relay.append(spread(5, lax.rem(x + 1, NX), 1, left))
        sends = sends + relay
        for s in sends[2:]:
            s.wait_recv()
        pending += sends
        if last:
            out[...] = fresh[it]
        else:
            words[:, :SUB] = fresh[it]
            for xx in range(NX):
                for q in range(XK // SUB):
                    at = pl.ds(xx * XK + q * SUB, SUB)
                    half = jnp.broadcast_to(normx[xx, q : q + 1, :], (SUB, SUB)).T
                    words[at, SUB:] = extra(half).astype(bf16)
    for s in pending:
        s.wait_send()


def vmem():
    return pl.BlockSpec(memory_space=pltpu.VMEM)


def exchange(samples, table, lut, assign):
    dma = pltpu.SemaphoreType.DMA
    return pl.pallas_call(
        exchange_kernel,
        out_shape=jax.ShapeDtypeStruct((ROWS, SUB), bf16),
        in_specs=[pl.BlockSpec(memory_space=pl.ANY), vmem(), vmem(), vmem()],
        out_specs=vmem(),
        scratch_shapes=[
            pltpu.VMEM((ROWS, SUB), bf16),
            pltpu.VMEM((NZ, 2, SUB, K // 2), bf16),
            pltpu.VMEM((NX, NZ, CAP), i32),
            pltpu.VMEM((NX, NZ, CAP), i32),
            pltpu.VMEM((NZ, NX - 1, SUB, CAP), bf16),
            pltpu.VMEM((NZ, NX, SUB, CAP), bf16),
            pltpu.VMEM((BLK, BLK), bf16),
            pltpu.VMEM((1, ROWS), i32),
            pltpu.VMEM((2 * NW, CAP), f32),
            pltpu.VMEM((SUB, ROWS), f32),
            dma((2,)), dma((7,)), dma((7,)), dma((7,)), dma((7,)), dma((7,)), dma((7,)),
            dma((3,)), dma((3,)), dma((NZ, 3)), dma((NZ, 3)),
        ],
        compiler_params=pltpu.CompilerParams(
            collective_id=0, has_side_effects=True, vmem_limit_bytes=48 << 20
        ),
        name="exchange",
    )(samples, table, lut, assign)


def refine(rows, book):
    dma = pltpu.SemaphoreType.DMA
    x3, z7, x6 = (ITERS, 3), (ITERS, 7), (ITERS, 6)
    return pl.pallas_call(
        em_kernel,
        out_shape=jax.ShapeDtypeStruct((K, SUB), bf16),
        in_specs=[vmem(), vmem()],
        out_specs=vmem(),
        scratch_shapes=[
            pltpu.VMEM((ROWS, 2 * SUB), bf16),
            pltpu.VMEM((ROWS, 2 * SUB), bf16),
            pltpu.VMEM((K, 2 * SUB), bf16),
            pltpu.VMEM((K, ROWS), bf16),
            pltpu.VMEM((K, RB), f32),
            pltpu.VMEM((K, RB), f32),
            pltpu.VMEM((ITERS, 6, XH, SUB), bf16),
            pltpu.VMEM((XK, SUB), f32),
            pltpu.VMEM((ITERS, 3, 8, SUB), f32),
            pltpu.VMEM((ITERS, 6, XH, SUB), bf16),
            pltpu.VMEM((ITERS, 3, 8, SUB), f32),
            pltpu.VMEM((ITERS, XK, SUB), bf16),
            pltpu.VMEM((ITERS, 8, SUB), f32),
            pltpu.VMEM((ITERS, 7, OWN, SUB), bf16),
            pltpu.VMEM((ITERS, 7, 8, SUB), f32),
            pltpu.VMEM((ITERS, K, SUB), bf16),
            pltpu.VMEM((8, SUB), f32),
            pltpu.VMEM((8, SUB), f32),
            pltpu.VMEM((NX + 7, 8, SUB), f32),
            pltpu.VMEM((OWN, SUB), f32),
            dma(x6), dma(x6), dma(x3), dma(x3), dma(z7), dma(z7), dma(z7), dma(z7),
            dma(z7), dma(z7), dma((7,)), dma((7,)), dma(x6), dma(x6), dma((3,)), dma((3,)),
        ],
        compiler_params=pltpu.CompilerParams(
            collective_id=1, has_side_effects=True, vmem_limit_bytes=56 << 20
        ),
        name="refine",
    )(rows, book)


def on_device(samples, centroid_table, owner, slot, assign, codebook):
    pos = (owner * K + slot).reshape(512, 128)
    lut = jnp.concatenate([(pos >> 8).T, (pos & 255).T], axis=0).astype(bf16)
    table = centroid_table.reshape(2, K // 2, SUB).transpose(0, 2, 1)
    residual = exchange(samples, table, lut, assign.reshape(1, ROWS))
    refined = refine(residual, codebook[0])
    return residual, refined.astype(f32)[None]


def solution(mesh):
    return jax.shard_map(
        on_device,
        mesh=mesh,
        in_specs=(
            P(("wide", "narrow"), None),
            P("wide", "narrow"),
            P(),
            P(),
            P("wide"),
            P("narrow", None, None),
        ),
        out_specs=(P("wide", "narrow"), P("narrow", None, None)),
        check_vma=False,
    )
```
